256 devices in a mesh: seq: 64 (over y, z_lo, x), mp: 4 (over z_hi, core).
Axes of the slice: x: 4, y: 4, z: 8 (z_hi: 2, z_lo: 4; z = z_hi * 4 + z_lo), core: 2. Of those that a mesh axis runs over, the one named last changes fastest.
Arguments:
- projected: bfloat16 [3, 8192, 8192], P(None, 'mp', 'seq'), may hold values from -6 to 6
- short_taps: float32 [3, 3, 8192], replicated, may hold values from -4 to 4
- skip_gain: float32 [8192], replicated, may hold values from -4 to 4
- residue: float32 [2048, 16], P('seq'), may hold values from -4 to 4
- decay_rate: float32 [2048, 16], P('seq'), may hold values from 6.1035156e-05 to 0.05
Outputs:
- gated: bfloat16 [8192, 8192], P('mp', 'seq')
The draws below stay inside these ranges and needn't reach their ends.
All inputs are finite; a program needn't handle non-finite values.
Results may differ from the reference program's by a relative error of at most 0.012.
Values may be sent and summed in bfloat16 or wider, within the bound.
No kernel may reach another device: no remote copies, remote signals or barrier semaphores. Data moves between devices by JAX's collectives and lax.ppermute only.
A program may use at most 128 MiB of HBM per device.

```python
import math
import jax
import jax.numpy as jnp
from jax import lax

C = 8192
FILTERS = 2048
STATE = 16
SEQ = 8192


def levels(stream_key, shape, pieces, low, top_value):
    factor_of, own = 1.0, jax.random.fold_in(stream_key, 6)
    for axis_at, blocks in pieces:
        draws = jnp.exp(jax.random.uniform(jax.random.fold_in(own, axis_at), (blocks,), jnp.float32, low / len(pieces), top_value / len(pieces)))
        factor_of = factor_of * jnp.repeat(draws, shape[axis_at] // blocks).reshape([-1 if axis == axis_at else 1 for axis in range(len(shape))])
    return factor_of


def bell_draw(stream_key, dims, width, reach, cuts=(), held_as=jnp.bfloat16):
    drawn = width * jax.random.normal(stream_key, dims, jnp.float32)
    if cuts:
        drawn = drawn * levels(stream_key, dims, cuts, -0.22, 0.18)
    return jnp.clip(drawn, -reach, reach).astype(held_as)


def setup_inputs(seed: int = 0) -> dict:
    seeds = jax.random.split(jax.random.key(seed), 6)
    return {
        "projected": bell_draw(seeds[0], (3, C, SEQ), 1.0, 6.0, ((1, 4), (2, 64))),
        "short_taps": bell_draw(seeds[1], (3, 3, C), 0.6, 4.0, (), jnp.float32),
        "skip_gain": bell_draw(seeds[2], (C,), 1.0, 4.0, (), jnp.float32),
        "residue": bell_draw(seeds[3], (FILTERS, STATE), 0.5, 4.0, ((0, 64),), jnp.float32),
        "decay_rate": jnp.clip(jnp.exp(math.log(0.05) - 6.7083283 * jax.random.uniform(seeds[4], (FILTERS, STATE), jnp.float32) ** levels(seeds[4], (FILTERS, STATE), ((0, 64),), -0.2, 0.2)), 6.103515625e-05, 0.05),
    }


def filter_kernel(residue_block, rate_block, length):
    positions = jnp.arange(length, dtype=jnp.float32)
    kernel = jnp.zeros((residue_block.shape[0], length), jnp.float32)
    for state_index in range(STATE):
        weight = residue_block[:, state_index] * jnp.sqrt(rate_block[:, state_index])
        kernel = kernel + weight[:, None] * jnp.exp(-rate_block[:, state_index][:, None] * positions[None, :])
    return kernel

def reference(projected, short_taps, skip_gain, residue, decay_rate):
    channels = projected.shape[1]
    length = projected.shape[2]
    block_size = math.gcd(512, FILTERS)
    block_count = channels // block_size

    def one_block(block_index):
        offset = (block_index * block_size).astype(jnp.int32)
        values = lax.dynamic_slice_in_dim(projected, offset, block_size, 1).astype(jnp.float32)
        tap_block = lax.dynamic_slice_in_dim(short_taps, offset, block_size, 2)
        padded = jnp.pad(values, ((0, 0), (0, 0), (2, 0)))
        mixed = tap_block[0][:, :, None] * values + tap_block[1][:, :, None] * padded[:, :, 1:-1] + tap_block[2][:, :, None] * padded[:, :, :-2]
        product = (mixed[1] * mixed[2]).astype(jnp.bfloat16)
        filter_start = (offset % FILTERS).astype(jnp.int32)
        residue_block = lax.dynamic_slice_in_dim(residue, filter_start, block_size, 0)
        rate_block = lax.dynamic_slice_in_dim(decay_rate, filter_start, block_size, 0)
        kernel = filter_kernel(residue_block, rate_block, length)
        spectrum = jnp.fft.rfft(product.astype(jnp.float32), n=2 * length) * jnp.fft.rfft(kernel, n=2 * length)
        long_part = jnp.fft.irfft(spectrum, n=2 * length)[:, :length].astype(jnp.bfloat16)
        skip_block = lax.dynamic_slice_in_dim(skip_gain, offset, block_size, 0)
        total = long_part.astype(jnp.float32) + skip_block[:, None] * product.astype(jnp.float32)
        return (mixed[0] * total).astype(jnp.bfloat16)
    gated = lax.map(one_block, jnp.arange(block_count, dtype=jnp.int32))
    return gated.reshape(channels, length)
```

```python
import math

import jax
import jax.numpy as jnp
import ml_dtypes
import numpy as np
from jax import lax
from jax.experimental import pallas as pl
from jax.experimental.pallas import tpu as pltpu
from jax.sharding import PartitionSpec as P

BLOCK = 128
MODES = 16
GROUP = 16
LANES = GROUP * MODES
f32 = jnp.float32
bf16 = jnp.bfloat16


def split_pair(value):
    high = value.astype(bf16)
    return high, (value - high.astype(f32)).astype(bf16)


def transform_tables():
    steps = np.arange(BLOCK, dtype=np.float64)
    angles = 2.0 * math.pi / BLOCK * np.outer(steps, steps - 0.25)
    table = np.concatenate([np.cos(angles), -np.sin(angles)], axis=1)
    high = table.astype(np.float32).astype(ml_dtypes.bfloat16)
    low = (table - high.astype(np.float64)).astype(np.float32).astype(ml_dtypes.bfloat16)
    return high, low


def mm(left, right):
    return lax.dot_general(left, right, (((1,), (0,)), ((), ())), preferred_element_type=f32)


def mm_nt(left, right, precision=None):
    return lax.dot_general(
        left, right, (((1,), (1,)), ((), ())), preferred_element_type=f32, precision=precision
    )


def halo_kernel(x_ref, out_ref):
    step = pl.program_id(0)
    lane = lax.broadcasted_iota(jnp.int32, (BLOCK, BLOCK), 1)

    @pl.when(step == 0)
    def _():
        out_ref[...] = jnp.zeros_like(out_ref)

    acc = jnp.zeros((BLOCK, BLOCK), f32)
    for part in range(4):
        for stream in range(3):
            tile = x_ref[stream, part * BLOCK : (part + 1) * BLOCK, :].astype(f32)
            slot = 8 * part + 2 * stream
            acc = jnp.where(
                (lane // 2) == slot // 2, pltpu.roll(tile, (slot - BLOCK + 2) % BLOCK, 1), acc
            )
    rolled = pltpu.roll(acc, step * 32, 1)
    out_ref[...] = jnp.where((lane // 32) == step, rolled, out_ref[...].astype(f32)).astype(bf16)


def pack_halo(projected):
    return pl.pallas_call(
        halo_kernel,
        grid=(4,),
        in_specs=[pl.BlockSpec((3, 512, BLOCK), lambda i: (0, i, 0))],
        out_specs=pl.BlockSpec((BLOCK, BLOCK), lambda i: (0, 0)),
        out_shape=jax.ShapeDtypeStruct((BLOCK, BLOCK), bf16),
        name="pack_halo",
    )(projected)


def short_mix(tile, before, taps, stream, lane):
    one = pltpu.roll(jnp.where(lane == BLOCK - 1, before, tile), 1, 1)
    two = pltpu.roll(jnp.where(lane >= BLOCK - 2, before, tile), 2, 1)
    return (
        taps[:, stream : stream + 1] * tile
        + taps[:, 3 + stream : 4 + stream] * one
        + taps[:, 6 + stream : 7 + stream] * two
    )


def tap_columns(taps_ref, span):
    rows = [taps_ref[lag, :, span] for lag in range(3)]
    rows.append(jnp.zeros((7, BLOCK), f32))
    return jnp.concatenate(rows, axis=0).T


def product_kernel(mp_ref, k_ref, v_ref, halo_ref, taps_ref, out_ref):
    step = pl.program_id(0)
    lane = lax.broadcasted_iota(jnp.int32, (BLOCK, BLOCK), 1)
    halo = halo_ref[...].astype(f32)
    for part in range(4):
        span = slice(part * BLOCK, (part + 1) * BLOCK)
        taps = tap_columns(taps_ref, span)
        place = step * 32 + part * 8
        k_before = pltpu.roll(halo, 2 * BLOCK - 4 - place, 1)
        v_before = pltpu.roll(halo, 2 * BLOCK - 6 - place, 1)
        k_mix = short_mix(k_ref[0, span, :].astype(f32), k_before, taps, 1, lane)
        v_mix = short_mix(v_ref[0, span, :].astype(f32), v_before, taps, 2, lane)
        out_ref[span, :] = (k_mix * v_mix).astype(bf16)


def make_product(projected, halo, short_taps, mp_index):
    stream_spec = lambda s: pl.BlockSpec((1, 512, BLOCK), lambda i, mp: (s, i, 0))
    return pl.pallas_call(
        product_kernel,
        grid_spec=pltpu.PrefetchScalarGridSpec(
            num_scalar_prefetch=1,
            grid=(4,),
            in_specs=[
                stream_spec(1),
                stream_spec(2),
                pl.BlockSpec((BLOCK, BLOCK), lambda i, mp: (0, 0)),
                pl.BlockSpec((3, 3, 512), lambda i, mp: (0, 0, mp[0] * 4 + i)),
            ],
            out_specs=pl.BlockSpec((512, BLOCK), lambda i, mp: (i, 0)),
        ),
        out_shape=jax.ShapeDtypeStruct((2048, BLOCK), bf16),
        name="product",
    )(mp_index, projected, projected, halo, short_taps)


def gate_kernel(mp_ref, q_ref, product_ref, long_ref, halo_ref, taps_ref, skip_ref, out_ref):
    step = pl.program_id(0)
    lane = lax.broadcasted_iota(jnp.int32, (BLOCK, BLOCK), 1)
    halo = halo_ref[...].astype(f32)
    for part in range(4):
        span = slice(part * BLOCK, (part + 1) * BLOCK)
        taps = tap_columns(taps_ref, span)
        skip = jnp.broadcast_to(skip_ref[:, span], (16, BLOCK)).T[:, 0:1]
        place = step * 32 + part * 8
        q_before = pltpu.roll(halo, 2 * BLOCK - 2 - place, 1)
        q_mix = short_mix(q_ref[0, span, :].astype(f32), q_before, taps, 0, lane)
        total = long_ref[span, :].astype(f32) + skip * product_ref[span, :].astype(f32)
        out_ref[span, :] = (q_mix * total).astype(bf16)


def apply_gate(projected, product, long_part, halo, short_taps, skip_gain, mp_index):
    rows = pl.BlockSpec((512, BLOCK), lambda i, mp: (i, 0))
    return pl.pallas_call(
        gate_kernel,
        grid_spec=pltpu.PrefetchScalarGridSpec(
            num_scalar_prefetch=1,
            grid=(4,),
            in_specs=[
                pl.BlockSpec((1, 512, BLOCK), lambda i, mp: (0, i, 0)),
                rows,
                rows,
                pl.BlockSpec((BLOCK, BLOCK), lambda i, mp: (0, 0)),
                pl.BlockSpec((3, 3, 512), lambda i, mp: (0, 0, mp[0] * 4 + i)),
                pl.BlockSpec((1, 512), lambda i, mp: (0, mp[0] * 4 + i)),
            ],
            out_specs=rows,
        ),
        out_shape=jax.ShapeDtypeStruct((2048, BLOCK), bf16),
        name="gate",
    )(mp_index, projected, product, long_part, halo, short_taps, skip_gain.reshape(1, -1))


def flat_row(values, groups):
    mode = lax.broadcasted_iota(jnp.int32, (MODES, LANES), 0)
    lane = lax.broadcasted_iota(jnp.int32, (MODES, LANES), 1)
    pick = (lane % MODES == mode).astype(f32)
    own = (lane // MODES) == mode
    spread = lax.dot_general(
        values, pick, (((1,), (0,)), ((), ())), preferred_element_type=f32,
        precision=lax.Precision.HIGHEST,
    )
    rows = [
        jnp.sum(jnp.where(own, spread[g * GROUP : (g + 1) * GROUP], 0.0), axis=0, keepdims=True)
        for g in range(groups)
    ]
    return jnp.concatenate(rows, axis=1)


def long_kernel(
    x_ref, residue_ref, rate_ref, high_ref, low_ref, out_ref,
    in_hi, in_lo, out_hi, out_lo, spec_ref, state_ref,
):
    blocks, channels, _ = x_ref.shape
    groups = channels // GROUP
    lanes = groups * LANES
    rate_row = flat_row(rate_ref[...], groups)
    weight_row = flat_row(residue_ref[...], groups) * jnp.sqrt(rate_row)
    place = lax.broadcasted_iota(jnp.int32, (BLOCK, lanes), 0).astype(f32)
    in_hi[...], in_lo[...] = split_pair(jnp.exp(-rate_row * (BLOCK - 1.0 - place)))
    weighted = weight_row * jnp.exp(-rate_row * place)
    out_hi[...], out_lo[...] = split_pair(weighted * jnp.exp(-rate_row))
    member = (
        lax.broadcasted_iota(jnp.int32, (channels, lanes), 1) // MODES
        == lax.broadcasted_iota(jnp.int32, (channels, lanes), 0)
    ).astype(f32)
    kernel = mm_nt(member, weighted, lax.Precision.HIGHEST)
    k_hi, k_lo = split_pair(kernel)
    spec_ref[...] = (
        mm(k_hi, high_ref[...]) + mm(k_hi, low_ref[...]) + mm(k_lo, high_ref[...])
    ) * (1.0 / BLOCK)

    own = (
        lax.broadcasted_iota(jnp.int32, (GROUP, LANES), 1) // MODES
        == lax.broadcasted_iota(jnp.int32, (GROUP, LANES), 0)
    )
    chunk = 8
    rows = chunk * GROUP

    def gather_states(i, carry):
        at = pl.multiple_of(i * chunk, chunk)
        for g in range(groups):
            x = x_ref[pl.ds(at, chunk), g * GROUP : (g + 1) * GROUP, :].reshape(rows, BLOCK)
            span = slice(g * LANES, (g + 1) * LANES)
            found = mm(x, in_hi[:, span]) + mm(x, in_lo[:, span])
            found = jnp.where(own, found.reshape(chunk, GROUP, LANES), 0.0)
            state_ref[pl.ds(at, chunk), span] = jnp.sum(found, axis=1)
        return carry

    lax.fori_loop(0, blocks // chunk, gather_states, 0)
    decay = jnp.exp(-float(BLOCK) * rate_row)
    state = jnp.zeros((1, lanes), f32)
    for b in range(blocks):
        ended = state_ref[b : b + 1, :]
        state_ref[b : b + 1, :] = state
        state = state * decay + ended

    def convolve(i, carry):
        at = pl.multiple_of(i * chunk, chunk)
        for g in range(groups):
            x = x_ref[pl.ds(at, chunk), g * GROUP : (g + 1) * GROUP, :].reshape(rows, BLOCK)
            span = slice(g * LANES, (g + 1) * LANES)
            turned = (mm(x, high_ref[...]) + mm(x, low_ref[...])).reshape(chunk, GROUP, 2 * BLOCK)
            x_re, x_im = turned[:, :, :BLOCK], turned[:, :, BLOCK:]
            spec = spec_ref[g * GROUP : (g + 1) * GROUP, :]
            k_re, k_im = spec[:, :BLOCK], spec[:, BLOCK:]
            mixed = jnp.concatenate(
                [x_re * k_re - x_im * k_im, x_re * k_im + x_im * k_re], axis=2
            ).reshape(rows, 2 * BLOCK)
            m_hi, m_lo = split_pair(mixed)
            state = jnp.where(own, state_ref[pl.ds(at, chunk), span][:, None, :], 0.0)
            s_hi, s_lo = split_pair(state.reshape(rows, LANES))
            result = (
                mm_nt(m_hi, high_ref[...]) + mm_nt(m_hi, low_ref[...]) + mm_nt(m_lo, high_ref[...])
            ) + (
                mm_nt(s_hi, out_hi[:, span]) + mm_nt(s_hi, out_lo[:, span]) + mm_nt(s_lo, out_hi[:, span])
            )
            out_ref[pl.ds(at, chunk), g * GROUP : (g + 1) * GROUP, :] = result.astype(bf16).reshape(
                chunk, GROUP, BLOCK
            )
        return carry

    lax.fori_loop(0, blocks // chunk, convolve, 0)


def long_convolve(blocks, residue, decay_rate):
    count, channels, _ = blocks.shape
    lanes = channels * MODES
    high, low = transform_tables()
    return pl.pallas_call(
        long_kernel,
        out_shape=jax.ShapeDtypeStruct(blocks.shape, bf16),
        scratch_shapes=[pltpu.VMEM((BLOCK, lanes), bf16)] * 4
        + [pltpu.VMEM((channels, 2 * BLOCK), f32), pltpu.VMEM((count, lanes), f32)],
        compiler_params=pltpu.CompilerParams(vmem_limit_bytes=32 << 20),
        name="long_conv",
    )(blocks, residue, decay_rate, jnp.asarray(high), jnp.asarray(low))


def body(projected, short_taps, skip_gain, residue, decay_rate):
    seq_count = lax.axis_size("seq")
    mp_index = lax.axis_index("mp").astype(jnp.int32).reshape(1)
    halo = lax.ppermute(
        pack_halo(projected), "seq", [(i, i + 1) for i in range(seq_count - 1)]
    )
    product = make_product(projected, halo, short_taps, mp_index)
    arrived = lax.all_to_all(
        product.reshape(seq_count, -1, BLOCK), "seq", split_axis=0, concat_axis=0, tiled=True
    )
    result = long_convolve(arrived, residue, decay_rate)
    long_part = lax.all_to_all(result, "seq", split_axis=0, concat_axis=0, tiled=True)
    return apply_gate(
        projected, product, long_part.reshape(product.shape), halo, short_taps, skip_gain, mp_index
    )


def solution(mesh):
    in_specs = (P(None, "mp", "seq"), P(), P(), P("seq", None), P("seq", None))
    out_specs = P("mp", "seq")
    return jax.shard_map(body, mesh=mesh, in_specs=in_specs, out_specs=out_specs, check_vma=False)
```

```python
import math

import jax
import jax.numpy as jnp
import ml_dtypes
import numpy as np
from jax import lax
from jax.experimental import pallas as pl
from jax.experimental.pallas import tpu as pltpu
from jax.sharding import Mesh, PartitionSpec as P

BLOCK = 128
MODES = 16
SIDE = 4
OWNERS = SIDE * SIDE
f32 = jnp.float32
bf16 = jnp.bfloat16
SMALL = pltpu.CompilerParams(vmem_limit_bytes=16 << 20)


def split_pair(value):
    high = value.astype(bf16)
    return high, (value - high.astype(f32)).astype(bf16)


def transform_tables():
    steps = np.arange(BLOCK, dtype=np.float64)
    angles = 2.0 * math.pi / BLOCK * np.outer(steps, steps - 0.25)
    table = np.concatenate([np.cos(angles), -np.sin(angles)], axis=1)
    high = table.astype(np.float32).astype(ml_dtypes.bfloat16)
    low = (table - high.astype(np.float64)).astype(np.float32).astype(ml_dtypes.bfloat16)
    forward = np.concatenate([high.T, low.T], axis=1)
    backward = np.concatenate([high, low], axis=0)
    return jnp.asarray(forward), jnp.asarray(backward)


def shift_table():
    row = lax.broadcasted_iota(jnp.int32, (BLOCK, BLOCK), 0)
    column = lax.broadcasted_iota(jnp.int32, (BLOCK, BLOCK), 1)
    return jnp.concatenate([(row - lag == column).astype(bf16) for lag in range(3)], axis=0)


def mm(left, right):
    return lax.dot_general(left, right, (((1,), (0,)), ((), ())), preferred_element_type=f32)


def mm_nt(left, right, precision=None):
    return lax.dot_general(
        left, right, (((1,), (1,)), ((), ())), preferred_element_type=f32, precision=precision
    )


def full(shape):
    return pl.BlockSpec(shape, lambda *_: (0,) * len(shape))


def owner_rows(x):
    return [slice(128 * zl + 32 * x, 128 * zl + 32 * x + 32) for zl in range(SIDE)]


def mix_kernel(
    mp_ref, x_ref, taps_ref, skip_ref, residue_ref, rate_ref,
    product_ref, gate_ref, head_ref, halo_ref, rows_ref, params_ref,
):
    shifts = shift_table()
    lane = lax.broadcasted_iota(jnp.int32, (16, BLOCK), 1) // 32
    table = jnp.concatenate(
        [taps_ref[0], taps_ref[1], taps_ref[2], skip_ref[...], jnp.zeros((6, 4 * BLOCK), f32)], axis=0
    )
    for x in range(SIDE):
        rows = jnp.zeros((16, BLOCK), f32)
        for zl in range(SIDE):
            piece = table[:, zl * BLOCK : (zl + 1) * BLOCK]
            if zl != x:
                piece = pltpu.roll(piece, (32 * (zl - x)) % BLOCK, 1)
            rows = jnp.where(lane == zl, piece, rows)
        rows_ref[x] = rows
        mixes = []
        for stream in range(3):
            tile = jnp.concatenate([x_ref[stream, span, :] for span in owner_rows(x)], axis=0)
            moved = mm_nt(shifts, tile)
            halo_ref[x, 2 * stream : 2 * stream + 2, :] = moved[BLOCK - 2 : BLOCK]
            mixes.append(
                rows[stream : stream + 1] * moved[:BLOCK]
                + rows[3 + stream : 4 + stream] * moved[BLOCK : 2 * BLOCK]
                + rows[6 + stream : 7 + stream] * moved[2 * BLOCK :]
            )
        halo_ref[x, 6:8, :] = jnp.zeros((2, BLOCK), f32)
        gate_ref[x] = mixes[0]
        head_ref[0, x] = mixes[1][:8]
        head_ref[1, x] = mixes[2][:8]
        product_ref[x] = (mixes[1] * mixes[2]).astype(bf16)

    @pl.when(pl.program_id(0) == 0)
    def _():
        rate = rate_ref[...]
        count = rate.shape[1]
        params_ref[...] = jnp.zeros((2 * MODES, BLOCK), f32)
        params_ref[:MODES, :count] = rate
        params_ref[MODES:, :count] = residue_ref[...] * jnp.sqrt(rate)


def mix_streams(projected, short_taps, skip_gain, residue, decay_rate, mp_index):
    tile = lambda n: pl.BlockSpec((4, n, BLOCK), lambda i, mp: (i, 0, 0))
    projected = pltpu.with_memory_space_constraint(projected, pltpu.HBM)
    short_taps = pltpu.with_memory_space_constraint(short_taps, pltpu.HBM)
    return pl.pallas_call(
        mix_kernel,
        grid_spec=pltpu.PrefetchScalarGridSpec(
            num_scalar_prefetch=1,
            grid=(4,),
            in_specs=[
                pl.BlockSpec((3, 512, BLOCK), lambda i, mp: (0, i, 0)),
                pl.BlockSpec((3, 3, 512), lambda i, mp: (0, 0, mp[0] * 4 + i)),
                pl.BlockSpec((1, 512), lambda i, mp: (0, mp[0] * 4 + i)),
                full(residue.shape[::-1]),
                full(decay_rate.shape[::-1]),
            ],
            out_specs=[
                tile(BLOCK),
                tile(BLOCK),
                pl.BlockSpec((2, 4, 8, BLOCK), lambda i, mp: (0, i, 0, 0)),
                tile(8),
                tile(16),
                full((2 * MODES, BLOCK)),
            ],
        ),
        out_shape=[
            jax.ShapeDtypeStruct((OWNERS, BLOCK, BLOCK), bf16),
            jax.ShapeDtypeStruct((OWNERS, BLOCK, BLOCK), f32),
            jax.ShapeDtypeStruct((2, OWNERS, 8, BLOCK), f32),
            jax.ShapeDtypeStruct((OWNERS, 8, BLOCK), f32),
            jax.ShapeDtypeStruct((OWNERS, 16, BLOCK), f32),
            jax.ShapeDtypeStruct((2 * MODES, BLOCK), f32),
        ],
        compiler_params=SMALL,
        name="mix",
    )(mp_index, projected, short_taps, skip_gain.reshape(1, -1), residue.T, decay_rate.T)


def halo_term(halo, rows, stream):
    at = lax.broadcasted_iota(jnp.int32, (8, BLOCK), 0)
    older = halo[2 * stream : 2 * stream + 1]
    newer = halo[2 * stream + 1 : 2 * stream + 2]
    one = rows[3 + stream : 4 + stream]
    two = rows[6 + stream : 7 + stream]
    return jnp.where(at == 0, one * newer + two * older, jnp.where(at == 1, two * newer, 0.0))


def head_kernel(product_ref, head_ref, halo_ref, rows_ref, out_ref):
    for g in range(OWNERS):
        halo = halo_ref[g]
        rows = rows_ref[g]
        k_mix = head_ref[0, g] + halo_term(halo, rows, 1)
        v_mix = head_ref[1, g] + halo_term(halo, rows, 2)
        rest = product_ref[g, 8:16, :].astype(f32)
        out_ref[g] = jnp.concatenate([k_mix * v_mix, rest], axis=0).astype(bf16)


def finish_product(product, head, halo, rows):
    top = pl.BlockSpec((OWNERS, 16, BLOCK), lambda i: (0, 0, 0))
    return pl.pallas_call(
        head_kernel,
        grid=(1,),
        in_specs=[top, full(head.shape), full(halo.shape), full(rows.shape)],
        out_specs=top,
        out_shape=jax.ShapeDtypeStruct(product.shape, bf16),
        input_output_aliases={0: 0},
        compiler_params=SMALL,
        name="head",
    )(product, head, halo, rows)


def gate_kernel(mix_ref, product_ref, long_ref, halo_ref, rows_ref, out_ref):
    for x in range(SIDE):
        mix = mix_ref[x]
        rows = rows_ref[x]
        mix = jnp.concatenate([mix[:8] + halo_term(halo_ref[x], rows, 0), mix[8:]], axis=0)
        total = long_ref[x].astype(f32) + rows[9:10] * product_ref[x].astype(f32)
        gated = (mix * total).T.astype(bf16)
        for zl, span in enumerate(owner_rows(x)):
            out_ref[span, :] = gated[32 * zl : 32 * zl + 32]


def apply_gate(mix, product, long_part, halo, rows):
    tile = lambda n: pl.BlockSpec((4, n, BLOCK), lambda i: (i, 0, 0))
    return pl.pallas_call(
        gate_kernel,
        grid=(4,),
        in_specs=[tile(BLOCK), tile(BLOCK), tile(BLOCK), tile(8), tile(16)],
        out_specs=pl.BlockSpec((512, BLOCK), lambda i: (i, 0)),
        out_shape=jax.ShapeDtypeStruct((OWNERS * BLOCK, BLOCK), bf16),
        compiler_params=SMALL,
        name="gate",
    )(mix, product, long_part, halo, rows)


def table_kernel(
    zl_ref, p0_ref, p1_ref, p2_ref, p3_ref, forward_ref,
    spec_ref, step_ref, tail_ref, start_ref, decay_ref,
):
    params = (
        p0_ref[...]
        + pltpu.roll(p1_ref[...], 32, 1)
        + pltpu.roll(p2_ref[...], 64, 1)
        + pltpu.roll(p3_ref[...], 96, 1)
    )
    params = pltpu.roll(params, zl_ref[0] * 32, 1)
    rate = params[:MODES]
    weight = params[MODES:]
    decay_ref[...] = jnp.exp(-float(BLOCK) * rate)
    place = lax.broadcasted_iota(jnp.int32, (BLOCK, BLOCK), 0).astype(f32)
    row = lax.broadcasted_iota(jnp.int32, (8, BLOCK), 0).astype(f32)
    kernel = jnp.zeros((BLOCK, BLOCK), f32)
    for n in range(MODES):
        own = rate[n : n + 1]
        gain = weight[n : n + 1]
        kernel = kernel + gain * jnp.exp(-own * place)
        step_ref[n] = jnp.broadcast_to(jnp.exp(-8.0 * own), (8, BLOCK))
        tail_ref[n] = jnp.exp(-own * (7.0 - row))
        start_ref[n] = gain * jnp.exp(-own * (row + 1.0))
    high, low = split_pair(kernel)
    table = forward_ref[...]
    spec = mm(table, jnp.concatenate([high, high], axis=0)) + mm(table[:, :BLOCK], low)
    spec = spec * (1.0 / BLOCK)
    spec_ref[...] = jnp.concatenate([spec, spec], axis=1)


def make_tables(pieces, forward, zl_index):
    part = jax.ShapeDtypeStruct((MODES, 8, BLOCK), f32)
    return pl.pallas_call(
        table_kernel,
        grid_spec=pltpu.PrefetchScalarGridSpec(
            num_scalar_prefetch=1,
            grid=(1,),
            in_specs=[full((2 * MODES, BLOCK))] * 4 + [full(forward.shape)],
            out_specs=[full((2 * BLOCK, 2 * BLOCK))] + [full(part.shape)] * 3 + [full((MODES, BLOCK))],
        ),
        out_shape=[
            jax.ShapeDtypeStruct((2 * BLOCK, 2 * BLOCK), f32), part, part, part,
            jax.ShapeDtypeStruct((MODES, BLOCK), f32),
        ],
        compiler_params=SMALL,
        name="tables",
    )(zl_index, *pieces, forward)


def state_kernel(x_ref, step_ref, tail_ref, decay_ref, state_ref, run_ref):
    step = step_ref[...]
    tail = tail_ref[...]

    def one_block(b, carry):
        x = x_ref[b].astype(f32)
        state = jnp.zeros((MODES, 8, BLOCK), f32)
        for i in range(BLOCK // 8):
            state = state * step + x[8 * i : 8 * i + 8][None]
        state_ref[b] = jnp.sum(state * tail, axis=1)
        return carry

    lax.fori_loop(0, OWNERS, one_block, 0)
    decay = decay_ref[...]
    for y in range(SIDE):
        run = state_ref[SIDE * y]
        for x in range(1, SIDE):
            run = run * decay + state_ref[SIDE * y + x]
        run_ref[y] = run


def block_states(blocks, step, tail, decay):
    return pl.pallas_call(
        state_kernel,
        out_shape=[
            jax.ShapeDtypeStruct((OWNERS, MODES, BLOCK), f32),
            jax.ShapeDtypeStruct((SIDE, MODES, BLOCK), f32),
        ],
        compiler_params=SMALL,
        name="states",
    )(blocks, step, tail, decay)


def conv_kernel(x_ref, spec_ref, forward_ref, backward_ref, out_ref):
    for pair in range(OWNERS // 2):
        x = jnp.concatenate([x_ref[2 * pair], x_ref[2 * pair + 1]], axis=1)
        turned = mm(forward_ref[...], jnp.concatenate([x, x], axis=0))
        x_re, x_im = turned[:BLOCK], turned[BLOCK:]
        k_re, k_im = spec_ref[:BLOCK, :], spec_ref[BLOCK:, :]
        mixed = jnp.concatenate([x_re * k_re - x_im * k_im, x_re * k_im + x_im * k_re], axis=0)
        high, low = split_pair(mixed)
        both = mm(backward_ref[...], high)
        result = both[:BLOCK] + both[BLOCK:] + mm(backward_ref[:BLOCK, :], low)
        out_ref[2 * pair] = result[:, :BLOCK]
        out_ref[2 * pair + 1] = result[:, BLOCK:]


def convolve_blocks(blocks, spec, forward, backward):
    return pl.pallas_call(
        conv_kernel,
        out_shape=jax.ShapeDtypeStruct(blocks.shape, f32),
        compiler_params=SMALL,
        name="conv",
    )(blocks, spec, forward, backward)


def readout_kernel(
    zl_ref, inner_ref, state_ref, r0_ref, r1_ref, r2_ref, r3_ref, step_ref, start_ref, decay_ref,
    out_ref, runs_ref, enter_ref,
):
    own = zl_ref[0]
    for k, ref in enumerate((r0_ref, r1_ref, r2_ref, r3_ref)):
        runs_ref[(own + k) % SIDE] = ref[...]
    decay = decay_ref[...]
    squared = decay * decay
    run_decay = squared * squared
    state = jnp.zeros((MODES, BLOCK), f32)
    for y in range(SIDE):
        for zl in range(SIDE):

            @pl.when(own == zl)
            def _(state=state, y=y):
                enter_ref[SIDE * y] = state

            state = state * run_decay + runs_ref[zl, y]
        inside = enter_ref[SIDE * y]
        for x in range(1, SIDE):
            inside = inside * decay + state_ref[SIDE * y + x - 1]
            enter_ref[SIDE * y + x] = inside
    step = step_ref[...]

    def one_block(b, carry):
        share = start_ref[...] * enter_ref[b][:, None, :]
        for i in range(BLOCK // 16):
            parts = []
            for half in range(2):
                at = 16 * i + 8 * half
                parts.append(inner_ref[b, at : at + 8, :] + jnp.sum(share, axis=0))
                share = share * step
            out_ref[b, 16 * i : 16 * i + 16, :] = jnp.concatenate(parts, axis=0).astype(bf16)
        return carry

    lax.fori_loop(0, OWNERS, one_block, 0)


def add_states(inner, states, runs, step, start, decay, zl_index):
    return pl.pallas_call(
        readout_kernel,
        grid_spec=pltpu.PrefetchScalarGridSpec(
            num_scalar_prefetch=1,
            grid=(1,),
            in_specs=[full(inner.shape), full(states.shape)]
            + [full((SIDE, MODES, BLOCK))] * 4
            + [full(step.shape)] * 2
            + [full(decay.shape)],
            out_specs=full(inner.shape),
            scratch_shapes=[
                pltpu.VMEM((SIDE, SIDE, MODES, BLOCK), f32),
                pltpu.VMEM((OWNERS, MODES, BLOCK), f32),
            ],
        ),
        out_shape=jax.ShapeDtypeStruct(inner.shape, bf16),
        compiler_params=SMALL,
        name="readout",
    )(zl_index, inner, states, *runs, step, start, decay)


def body(projected, short_taps, skip_gain, residue, decay_rate):
    mp_index = lax.axis_index("mp").astype(jnp.int32).reshape(1)
    zl_index = lax.axis_index("zl").astype(jnp.int32).reshape(1)
    count = SIDE ** 3

    def from_zl(value, k):
        return lax.ppermute(value, "zl", [(zl, (zl - k) % SIDE) for zl in range(SIDE)])

    product, gate_mix, head, halo, rows, params = mix_streams(
        projected, short_taps, skip_gain, residue, decay_rate, mp_index
    )
    halo = lax.ppermute(halo, ("y", "zl", "x"), [(i, i + 1) for i in range(count - 1)])
    pieces = [params] + [from_zl(params, k) for k in range(1, SIDE)]
    product = finish_product(product, head, halo, rows)
    product, *pieces = lax.optimization_barrier((product, *pieces))
    blocks = lax.all_to_all(product, ("y", "x"), split_axis=0, concat_axis=0, tiled=True)
    forward, backward = transform_tables()
    spec, step, tail, start, decay = make_tables(pieces, forward, zl_index)
    states, run = block_states(blocks, step, tail, decay)
    runs = [run] + [from_zl(run, k) for k in range(1, SIDE)]
    inner = convolve_blocks(blocks, spec, forward, backward)
    result = add_states(inner, states, runs, step, start, decay, zl_index)
    long_part = lax.all_to_all(result, ("y", "x"), split_axis=0, concat_axis=0, tiled=True)
    return apply_gate(gate_mix, product, long_part, halo, rows)


def solution(mesh):
    split = Mesh(mesh.devices.reshape(SIDE, SIDE, SIDE, -1), ("y", "zl", "x", "mp"))
    seq = ("y", "zl", "x")
    in_specs = (P(None, "mp", seq), P(), P(), P(seq, None), P(seq, None))
    out_specs = P("mp", seq)
    return jax.shard_map(body, mesh=split, in_specs=in_specs, out_specs=out_specs, check_vma=False)
```

```python
import math

import jax
import jax.numpy as jnp
import ml_dtypes
import numpy as np
from jax import lax
from jax.experimental import pallas as pl
from jax.experimental.pallas import tpu as pltpu
from jax.sharding import Mesh, PartitionSpec as P

BLOCK = 128
MODES = 16
SIDE = 4
OWNERS = SIDE * SIDE
f32 = jnp.float32
bf16 = jnp.bfloat16
SMALL = pltpu.CompilerParams(vmem_limit_bytes=16 << 20)


def split_pair(value):
    high = value.astype(bf16)
    return high, (value - high.astype(f32)).astype(bf16)


def transform_tables():
    steps = np.arange(BLOCK, dtype=np.float64)
    angles = 2.0 * math.pi / BLOCK * np.outer(steps, steps - 0.25)
    table = np.concatenate([np.cos(angles), -np.sin(angles)], axis=1)
    high = table.astype(np.float32).astype(ml_dtypes.bfloat16)
    low = (table - high.astype(np.float64)).astype(np.float32).astype(ml_dtypes.bfloat16)
    forward = np.concatenate([high.T, low.T], axis=1)
    backward = np.concatenate([high, low], axis=0)
    return jnp.asarray(forward), jnp.asarray(backward)


def shift_table():
    row = lax.broadcasted_iota(jnp.int32, (BLOCK, BLOCK), 0)
    column = lax.broadcasted_iota(jnp.int32, (BLOCK, BLOCK), 1)
    return jnp.concatenate([(row - lag == column).astype(bf16) for lag in range(3)], axis=0)


def mm(left, right):
    return lax.dot_general(left, right, (((1,), (0,)), ((), ())), preferred_element_type=f32)


def mm_nt(left, right, precision=None):
    return lax.dot_general(
        left, right, (((1,), (1,)), ((), ())), preferred_element_type=f32, precision=precision
    )


def full(shape):
    return pl.BlockSpec(shape, lambda *_: (0,) * len(shape))


def short_mix(moved, rows, stream):
    return (
        rows[stream : stream + 1] * moved[:BLOCK]
        + rows[3 + stream : 4 + stream] * moved[BLOCK : 2 * BLOCK]
        + rows[6 + stream : 7 + stream] * moved[2 * BLOCK :]
    )


def owner_rows(g):
    first = 512 * (g // SIDE) + 32 * (g % SIDE)
    return [slice(first + 128 * zl, first + 128 * zl + 32) for zl in range(SIDE)]


def mix_kernel(
    mp_ref, x_hbm, taps_hbm, skip_hbm, residue_hbm, rate_hbm,
    product_hbm, head_ref, halo_ref, rows_ref, params_ref,
    x_ref, taps_ref, skip_ref, residue_ref, rate_ref, product_ref, small_sems, x_sems, out_sems,
):
    span = OWNERS * BLOCK
    at = pl.multiple_of(mp_ref[0] * span, span)
    small = [
        pltpu.make_async_copy(source, target, small_sems.at[i])
        for i, (source, target) in enumerate(
            (
                (taps_hbm.at[:, :, pl.ds(at, span)], taps_ref),
                (skip_hbm.at[:, pl.ds(at, span)], skip_ref),
                (residue_hbm, residue_ref),
                (rate_hbm, rate_ref),
            )
        )
    ]
    large = [
        [
            pltpu.make_async_copy(
                x_hbm.at[stream, pl.ds(512 * y, 512)],
                x_ref.at[stream, pl.ds(512 * y, 512)],
                x_sems.at[y, stream],
            )
            for stream in range(3)
        ]
        for y in range(SIDE)
    ]
    out = [
        pltpu.make_async_copy(
            product_ref.at[pl.ds(SIDE * y, SIDE)], product_hbm.at[pl.ds(SIDE * y, SIDE)], out_sems.at[y]
        )
        for y in range(SIDE)
    ]
    for copy in small[:2] + large[0] + large[1] + large[2] + large[3] + small[2:]:
        copy.start()
    shifts = shift_table()
    last = lax.broadcasted_iota(jnp.int32, (16, BLOCK), 0) + (BLOCK - 2)
    last = (last == lax.broadcasted_iota(jnp.int32, (16, BLOCK), 1)).astype(bf16)
    lane = lax.broadcasted_iota(jnp.int32, (16, BLOCK), 1) // 32
    small[0].wait()
    small[1].wait()
    for y in range(SIDE):
        table = jnp.concatenate(
            [taps_ref[lag, :, 512 * y : 512 * y + 512] for lag in range(3)]
            + [skip_ref[:, 512 * y : 512 * y + 512], jnp.zeros((6, 4 * BLOCK), f32)],
            axis=0,
        )
        for copy in large[y]:
            copy.wait()
        for x in range(SIDE):
            g = SIDE * y + x
            rows = jnp.zeros((16, BLOCK), f32)
            for zl in range(SIDE):
                piece = table[:, zl * BLOCK : (zl + 1) * BLOCK]
                if zl != x:
                    piece = pltpu.roll(piece, (32 * (zl - x)) % BLOCK, 1)
                rows = jnp.where(lane == zl, piece, rows)
            rows_ref[g] = rows
            tiles = [
                jnp.concatenate([x_ref[stream, span, :] for span in owner_rows(g)], axis=0)
                for stream in range(3)
            ]
            halo_ref[g, 0:2, :] = mm_nt(last, tiles[0])[0:2]
            mixes = []
            for stream in (1, 2):
                moved = mm_nt(shifts, tiles[stream])
                halo_ref[g, 2 * stream : 2 * stream + 2, :] = moved[BLOCK - 2 : BLOCK]
                mixes.append(short_mix(moved, rows, stream))
                head_ref[stream - 1, g] = mixes[-1][:16]
            halo_ref[g, 6:8, :] = jnp.zeros((2, BLOCK), f32)
            product_ref[g] = (mixes[0] * mixes[1]).astype(bf16)
        out[y].start()
    small[2].wait()
    small[3].wait()
    rate = rate_ref[...]
    count = rate.shape[1]
    params_ref[...] = jnp.zeros((2 * MODES, BLOCK), f32)
    params_ref[:MODES, :count] = rate
    params_ref[MODES:, :count] = residue_ref[...] * jnp.sqrt(rate)
    for copy in out:
        copy.wait()


def in_hbm(value):
    return pltpu.with_memory_space_constraint(value, pltpu.HBM)


def mix_streams(projected, short_taps, skip_gain, residue, decay_rate, mp_index):
    span = OWNERS * BLOCK
    anywhere = pl.BlockSpec(memory_space=pl.ANY)
    whole = pl.BlockSpec(memory_space=pltpu.VMEM)
    mode_shape = residue.shape[::-1]
    return pl.pallas_call(
        mix_kernel,
        in_specs=[pl.BlockSpec(memory_space=pltpu.SMEM)] + [anywhere] * 5,
        out_specs=[anywhere] + [whole] * 4,
        out_shape=[
            jax.ShapeDtypeStruct((OWNERS, BLOCK, BLOCK), bf16),
            jax.ShapeDtypeStruct((2, OWNERS, 16, BLOCK), f32),
            jax.ShapeDtypeStruct((OWNERS, 8, BLOCK), f32),
            jax.ShapeDtypeStruct((OWNERS, 16, BLOCK), f32),
            jax.ShapeDtypeStruct((2 * MODES, BLOCK), f32),
        ],
        scratch_shapes=[
            pltpu.VMEM(projected.shape, bf16),
            pltpu.VMEM((3, 3, span), f32),
            pltpu.VMEM((1, span), f32),
            pltpu.VMEM(mode_shape, f32),
            pltpu.VMEM(mode_shape, f32),
            pltpu.VMEM((OWNERS, BLOCK, BLOCK), bf16),
            pltpu.SemaphoreType.DMA((4,)),
            pltpu.SemaphoreType.DMA((SIDE, 3)),
            pltpu.SemaphoreType.DMA((SIDE,)),
        ],
        compiler_params=SMALL,
        name="mix",
    )(
        mp_index, in_hbm(projected), in_hbm(short_taps), in_hbm(skip_gain.reshape(1, -1)),
        in_hbm(residue.T), in_hbm(decay_rate.T),
    )


def halo_term(halo, rows, stream):
    at = lax.broadcasted_iota(jnp.int32, (16, BLOCK), 0)
    older = halo[2 * stream : 2 * stream + 1]
    newer = halo[2 * stream + 1 : 2 * stream + 2]
    one = rows[3 + stream : 4 + stream]
    two = rows[6 + stream : 7 + stream]
    return jnp.where(at == 0, one * newer + two * older, jnp.where(at == 1, two * newer, 0.0))


def head_kernel(product_ref, head_ref, halo_ref, rows_ref, out_ref):
    del product_ref
    for g in range(OWNERS):
        halo = halo_ref[g]
        rows = rows_ref[g]
        k_mix = head_ref[0, g] + halo_term(halo, rows, 1)
        v_mix = head_ref[1, g] + halo_term(halo, rows, 2)
        out_ref[g] = (k_mix * v_mix).astype(bf16)


def finish_product(product, head, halo, rows):
    return pl.pallas_call(
        head_kernel,
        grid=(1,),
        in_specs=[
            pl.BlockSpec(memory_space=pl.ANY), full(head.shape), full(halo.shape), full(rows.shape)
        ],
        out_specs=pl.BlockSpec((OWNERS, 16, BLOCK), lambda i: (0, 0, 0)),
        out_shape=jax.ShapeDtypeStruct(product.shape, bf16),
        input_output_aliases={0: 0},
        compiler_params=SMALL,
        name="head",
    )(product, head, halo, rows)


def prepare_kernel(q_ref, product_ref, halo_ref, rows_ref, mix_ref, direct_ref):
    shifts = shift_table()
    for x in range(SIDE):
        rows = rows_ref[x]
        tile = jnp.concatenate([q_ref[0, span, :] for span in owner_rows(x)], axis=0)
        mix = short_mix(mm_nt(shifts, tile), rows, 0)
        mix_ref[x, :16, :] = mix[:16] + halo_term(halo_ref[x], rows, 0)
        mix_ref[x, 16:, :] = mix[16:]
        direct_ref[x] = rows[9:10] * product_ref[x].astype(f32)


def prepare_gate(projected, product, halo, rows):
    tile = lambda n: pl.BlockSpec((4, n, BLOCK), lambda i: (i, 0, 0))
    return pl.pallas_call(
        prepare_kernel,
        grid=(4,),
        in_specs=[
            pl.BlockSpec((1, 512, BLOCK), lambda i: (0, i, 0)), tile(BLOCK), tile(8), tile(16)
        ],
        out_specs=[tile(BLOCK), tile(BLOCK)],
        out_shape=[jax.ShapeDtypeStruct(product.shape, f32)] * 2,
        compiler_params=SMALL,
        name="prepare",
    )(in_hbm(projected), product, halo, rows)


def gate_kernel(mix_ref, direct_ref, long_ref, out_hbm, out_ref, sems):
    copies = [
        pltpu.make_async_copy(
            out_ref.at[pl.ds(512 * y, 512)], out_hbm.at[pl.ds(512 * y, 512)], sems.at[y]
        )
        for y in range(SIDE)
    ]
    for g in range(OWNERS):
        gated = (mix_ref[g] * (long_ref[g].astype(f32) + direct_ref[g])).astype(bf16).T
        for zl, span in enumerate(owner_rows(g)):
            out_ref[span, :] = gated[32 * zl : 32 * zl + 32]
        if g % SIDE == SIDE - 1:
            copies[g // SIDE].start()
    for copy in copies:
        copy.wait()


def apply_gate(mix, direct, long_part):
    shape = (OWNERS * BLOCK, BLOCK)
    return pl.pallas_call(
        gate_kernel,
        in_specs=[pl.BlockSpec(memory_space=pltpu.VMEM)] * 3,
        out_specs=pl.BlockSpec(memory_space=pl.ANY),
        out_shape=jax.ShapeDtypeStruct(shape, bf16),
        scratch_shapes=[pltpu.VMEM(shape, bf16), pltpu.SemaphoreType.DMA((SIDE,))],
        compiler_params=SMALL,
        name="gate",
    )(mix, direct, long_part)


def table_kernel(
    zl_ref, p0_ref, p1_ref, p2_ref, p3_ref, forward_ref,
    spec_ref, step_ref, tail_ref, start_ref, decay_ref,
):
    params = (
        p0_ref[...]
        + pltpu.roll(p1_ref[...], 32, 1)
        + pltpu.roll(p2_ref[...], 64, 1)
        + pltpu.roll(p3_ref[...], 96, 1)
    )
    params = pltpu.roll(params, zl_ref[0] * 32, 1)
    rate = params[:MODES]
    weight = params[MODES:]
    decay_ref[...] = jnp.exp(-float(BLOCK) * rate)
    place = lax.broadcasted_iota(jnp.int32, (BLOCK, BLOCK), 0).astype(f32)
    row = lax.broadcasted_iota(jnp.int32, (8, BLOCK), 0).astype(f32)
    kernel = jnp.zeros((BLOCK, BLOCK), f32)
    for n in range(MODES):
        own = rate[n : n + 1]
        gain = weight[n : n + 1]
        kernel = kernel + gain * jnp.exp(-own * place)
        step_ref[n] = jnp.broadcast_to(jnp.exp(-8.0 * own), (8, BLOCK))
        tail_ref[n] = jnp.exp(-own * (7.0 - row))
        start_ref[n] = gain * jnp.exp(-own * (row + 1.0))
    high, low = split_pair(kernel)
    table = forward_ref[...]
    spec = mm(table, jnp.concatenate([high, high], axis=0)) + mm(table[:, :BLOCK], low)
    spec = spec * (1.0 / BLOCK)
    spec_ref[...] = jnp.concatenate([spec, spec], axis=1)


def make_tables(pieces, forward, zl_index):
    part = jax.ShapeDtypeStruct((MODES, 8, BLOCK), f32)
    return pl.pallas_call(
        table_kernel,
        grid_spec=pltpu.PrefetchScalarGridSpec(
            num_scalar_prefetch=1,
            grid=(1,),
            in_specs=[full((2 * MODES, BLOCK))] * 4 + [full(forward.shape)],
            out_specs=[full((2 * BLOCK, 2 * BLOCK))] + [full(part.shape)] * 3 + [full((MODES, BLOCK))],
        ),
        out_shape=[
            jax.ShapeDtypeStruct((2 * BLOCK, 2 * BLOCK), f32), part, part, part,
            jax.ShapeDtypeStruct((MODES, BLOCK), f32),
        ],
        compiler_params=SMALL,
        name="tables",
    )(zl_index, *pieces, forward)


def state_kernel(x_ref, step_ref, tail_ref, decay_ref, state_ref, run_ref):
    step = step_ref[...]
    tail = tail_ref[...]

    def one_block(b, carry):
        x = x_ref[b].astype(f32)
        state = jnp.zeros((MODES, 8, BLOCK), f32)
        for i in range(BLOCK // 8):
            state = state * step + x[8 * i : 8 * i + 8][None]
        state_ref[b] = jnp.sum(state * tail, axis=1)
        return carry

    lax.fori_loop(0, OWNERS, one_block, 0)
    decay = decay_ref[...]
    for y in range(SIDE):
        run = state_ref[SIDE * y]
        for x in range(1, SIDE):
            run = run * decay + state_ref[SIDE * y + x]
        run_ref[y] = run


def block_states(blocks, step, tail, decay):
    return pl.pallas_call(
        state_kernel,
        out_shape=[
            jax.ShapeDtypeStruct((OWNERS, MODES, BLOCK), f32),
            jax.ShapeDtypeStruct((SIDE, MODES, BLOCK), f32),
        ],
        compiler_params=SMALL,
        name="states",
    )(blocks, step, tail, decay)


def conv_kernel(x_ref, spec_ref, forward_ref, backward_ref, out_ref):
    for pair in range(OWNERS // 2):
        x = jnp.concatenate([x_ref[2 * pair], x_ref[2 * pair + 1]], axis=1)
        turned = mm(forward_ref[...], jnp.concatenate([x, x], axis=0))
        x_re, x_im = turned[:BLOCK], turned[BLOCK:]
        k_re, k_im = spec_ref[:BLOCK, :], spec_ref[BLOCK:, :]
        mixed = jnp.concatenate([x_re * k_re - x_im * k_im, x_re * k_im + x_im * k_re], axis=0)
        high, low = split_pair(mixed)
        both = mm(backward_ref[...], high)
        result = both[:BLOCK] + both[BLOCK:] + mm(backward_ref[:BLOCK, :], low)
        out_ref[2 * pair] = result[:, :BLOCK]
        out_ref[2 * pair + 1] = result[:, BLOCK:]


def convolve_blocks(blocks, spec, forward, backward):
    return pl.pallas_call(
        conv_kernel,
        out_shape=jax.ShapeDtypeStruct(blocks.shape, f32),
        compiler_params=SMALL,
        name="conv",
    )(blocks, spec, forward, backward)


def readout_kernel(
    zl_ref, inner_ref, state_ref, r0_ref, r1_ref, r2_ref, r3_ref, step_ref, start_ref, decay_ref,
    out_ref, runs_ref, enter_ref,
):
    own = zl_ref[0]
    for k, ref in enumerate((r0_ref, r1_ref, r2_ref, r3_ref)):
        runs_ref[(own + k) % SIDE] = ref[...]
    decay = decay_ref[...]
    squared = decay * decay
    run_decay = squared * squared
    state = jnp.zeros((MODES, BLOCK), f32)
    for y in range(SIDE):
        for zl in range(SIDE):

            @pl.when(own == zl)
            def _(state=state, y=y):
                enter_ref[SIDE * y] = state

            state = state * run_decay + runs_ref[zl, y]
        inside = enter_ref[SIDE * y]
        for x in range(1, SIDE):
            inside = inside * decay + state_ref[SIDE * y + x - 1]
            enter_ref[SIDE * y + x] = inside
    step = step_ref[...]

    def one_block(b, carry):
        share = start_ref[...] * enter_ref[b][:, None, :]
        for i in range(BLOCK // 16):
            parts = []
            for half in range(2):
                at = 16 * i + 8 * half
                parts.append(inner_ref[b, at : at + 8, :] + jnp.sum(share, axis=0))
                share = share * step
            out_ref[b, 16 * i : 16 * i + 16, :] = jnp.concatenate(parts, axis=0).astype(bf16)
        return carry

    lax.fori_loop(0, OWNERS, one_block, 0)


def add_states(inner, states, runs, step, start, decay, zl_index):
    return pl.pallas_call(
        readout_kernel,
        grid_spec=pltpu.PrefetchScalarGridSpec(
            num_scalar_prefetch=1,
            grid=(1,),
            in_specs=[full(inner.shape), full(states.shape)]
            + [full((SIDE, MODES, BLOCK))] * 4
            + [full(step.shape)] * 2
            + [full(decay.shape)],
            out_specs=full(inner.shape),
            scratch_shapes=[
                pltpu.VMEM((SIDE, SIDE, MODES, BLOCK), f32),
                pltpu.VMEM((OWNERS, MODES, BLOCK), f32),
            ],
        ),
        out_shape=jax.ShapeDtypeStruct(inner.shape, bf16),
        compiler_params=SMALL,
        name="readout",
    )(zl_index, inner, states, *runs, step, start, decay)


def body(projected, short_taps, skip_gain, residue, decay_rate):
    mp_index = lax.axis_index("mp").astype(jnp.int32).reshape(1)
    zl_index = lax.axis_index("zl").astype(jnp.int32).reshape(1)
    count = SIDE ** 3

    def from_zl(value, k):
        return lax.ppermute(value, "zl", [(zl, (zl - k) % SIDE) for zl in range(SIDE)])

    product, head, halo, rows, params = mix_streams(
        projected, short_taps, skip_gain, residue, decay_rate, mp_index
    )
    halo = lax.ppermute(halo, ("y", "zl", "x"), [(i, i + 1) for i in range(count - 1)])
    pieces = [params] + [from_zl(params, k) for k in range(1, SIDE)]
    product = finish_product(product, head, halo, rows)
    product, *pieces = lax.optimization_barrier((product, *pieces))
    blocks = lax.all_to_all(product, ("y", "x"), split_axis=0, concat_axis=0, tiled=True)
    gate_mix, direct = prepare_gate(projected, product, halo, rows)
    blocks, gate_mix, direct = lax.optimization_barrier((blocks, gate_mix, direct))
    forward, backward = transform_tables()
    spec, step, tail, start, decay = make_tables(pieces, forward, zl_index)
    states, run = block_states(blocks, step, tail, decay)
    runs = [run] + [from_zl(run, k) for k in range(1, SIDE)]
    inner = convolve_blocks(blocks, spec, forward, backward)
    result = add_states(inner, states, runs, step, start, decay, zl_index)
    long_part = lax.all_to_all(result, ("y", "x"), split_axis=0, concat_axis=0, tiled=True)
    return apply_gate(gate_mix, direct, long_part)


def solution(mesh):
    split = Mesh(mesh.devices.reshape(SIDE, SIDE, SIDE, -1), ("y", "zl", "x", "mp"))
    seq = ("y", "zl", "x")
    in_specs = (P(None, "mp", seq), P(), P(), P(seq, None), P(seq, None))
    out_specs = P("mp", seq)
    return jax.shard_map(body, mesh=split, in_specs=in_specs, out_specs=out_specs, check_vma=False)
```

```python
import math

import jax
import jax.numpy as jnp
import ml_dtypes
import numpy as np
from jax import lax
from jax.experimental import pallas as pl
from jax.experimental.pallas import tpu as pltpu
from jax.sharding import Mesh, PartitionSpec as P

BLOCK = 128
MODES = 16
SIDE = 4
OWNERS = SIDE * SIDE
f32 = jnp.float32
bf16 = jnp.bfloat16
SMALL = pltpu.CompilerParams(vmem_limit_bytes=16 << 20)


def split_pair(value):
    high = value.astype(bf16)
    return high, (value - high.astype(f32)).astype(bf16)


def transform_tables():
    steps = np.arange(BLOCK, dtype=np.float64)
    angles = 2.0 * math.pi / BLOCK * np.outer(steps, steps - 0.25)
    table = np.concatenate([np.cos(angles), -np.sin(angles)], axis=1)
    high = table.astype(np.float32).astype(ml_dtypes.bfloat16)
    low = (table - high.astype(np.float64)).astype(np.float32).astype(ml_dtypes.bfloat16)
    forward = np.concatenate([high.T, low.T], axis=1)
    backward = np.concatenate([high, low], axis=0)
    return jnp.asarray(forward), jnp.asarray(backward)


def mm(left, right):
    return lax.dot_general(left, right, (((1,), (0,)), ((), ())), preferred_element_type=f32)


def mm_nt(left, right, precision=None):
    return lax.dot_general(
        left, right, (((1,), (1,)), ((), ())), preferred_element_type=f32, precision=precision
    )


def full(shape):
    return pl.BlockSpec(shape, lambda *_: (0,) * len(shape))


def later(value, steps):
    moved = pltpu.roll(value, steps, 0)
    row = lax.broadcasted_iota(jnp.int32, (8, BLOCK), 0)
    return jnp.concatenate([jnp.where(row < steps, 0.0, moved[:8]), moved[8:]], axis=0)


def short_mix(block, rows, stream):
    return (
        rows[stream : stream + 1] * block
        + rows[3 + stream : 4 + stream] * later(block, 1)
        + rows[6 + stream : 7 + stream] * later(block, 2)
    )


def owner_rows(g):
    first = 512 * (g // SIDE) + 32 * (g % SIDE)
    return [slice(first + 128 * zl, first + 128 * zl + 32) for zl in range(SIDE)]


def owner_tile(x_ref, stream, g):
    return jnp.concatenate([x_ref[stream, span, :] for span in owner_rows(g)], axis=0)


def mix_kernel(
    mp_ref, x_hbm, taps_hbm, skip_hbm, residue_hbm, rate_hbm,
    product_hbm, head_ref, halo_ref, rows_ref, params_ref,
    x_ref, taps_ref, skip_ref, residue_ref, rate_ref, product_ref, small_sems, x_sems, out_sems,
):
    span = OWNERS * BLOCK
    at = pl.multiple_of(mp_ref[0] * span, span)
    small = [
        pltpu.make_async_copy(source, target, small_sems.at[i])
        for i, (source, target) in enumerate(
            (
                (taps_hbm.at[:, :, pl.ds(at, span)], taps_ref),
                (skip_hbm.at[:, pl.ds(at, span)], skip_ref),
                (residue_hbm, residue_ref),
                (rate_hbm, rate_ref),
            )
        )
    ]
    large = [
        [
            pltpu.make_async_copy(
                x_hbm.at[stream, pl.ds(512 * y, 512)],
                x_ref.at[stream, pl.ds(512 * y, 512)],
                x_sems.at[y, stream],
            )
            for stream in range(3)
        ]
        for y in range(SIDE)
    ]
    out = [
        pltpu.make_async_copy(
            product_ref.at[pl.ds(SIDE * y, SIDE)], product_hbm.at[pl.ds(SIDE * y, SIDE)], out_sems.at[y]
        )
        for y in range(SIDE)
    ]
    inner = [large[y][stream] for y in range(SIDE) for stream in (1, 2)]
    outer = [large[y][0] for y in range(SIDE)]
    for copy in small[:2] + inner + outer + small[2:]:
        copy.start()
    lane = lax.broadcasted_iota(jnp.int32, (16, BLOCK), 1) // 32
    small[0].wait()
    small[1].wait()
    for y in range(SIDE):
        table = jnp.concatenate(
            [taps_ref[lag, :, 512 * y : 512 * y + 512] for lag in range(3)]
            + [skip_ref[:, 512 * y : 512 * y + 512], jnp.zeros((6, 4 * BLOCK), f32)],
            axis=0,
        )
        for x in range(SIDE):
            rows = jnp.zeros((16, BLOCK), f32)
            for zl in range(SIDE):
                piece = table[:, zl * BLOCK : (zl + 1) * BLOCK]
                if zl != x:
                    piece = pltpu.roll(piece, (32 * (zl - x)) % BLOCK, 1)
                rows = jnp.where(lane == zl, piece, rows)
            rows_ref[SIDE * y + x] = rows
    for y in range(SIDE):
        large[y][1].wait()
        large[y][2].wait()
        for g in range(SIDE * y, SIDE * y + SIDE):
            rows = rows_ref[g]
            mixes = []
            for stream in (1, 2):
                block = owner_tile(x_ref, stream, g).T.astype(f32)
                halo_ref[g, 2 * stream : 2 * stream + 2, :] = block[BLOCK - 2 :]
                mixes.append(short_mix(block, rows, stream))
                head_ref[stream - 1, g] = mixes[-1][:16]
            product_ref[g] = (mixes[0] * mixes[1]).astype(bf16)
        out[y].start()
    last = lax.broadcasted_iota(jnp.int32, (16, BLOCK), 0) + (BLOCK - 2)
    last = (last == lax.broadcasted_iota(jnp.int32, (16, BLOCK), 1)).astype(bf16)
    for y in range(SIDE):
        large[y][0].wait()
        for g in range(SIDE * y, SIDE * y + SIDE):
            halo_ref[g, 0:2, :] = mm_nt(last, owner_tile(x_ref, 0, g))[0:2]
            halo_ref[g, 6:8, :] = jnp.zeros((2, BLOCK), f32)
    small[2].wait()
    small[3].wait()
    rate = rate_ref[...]
    count = rate.shape[1]
    params_ref[...] = jnp.zeros((2 * MODES, BLOCK), f32)
    params_ref[:MODES, :count] = rate
    params_ref[MODES:, :count] = residue_ref[...] * jnp.sqrt(rate)
    for copy in out:
        copy.wait()


def in_hbm(value):
    return pltpu.with_memory_space_constraint(value, pltpu.HBM)


def mix_streams(projected, short_taps, skip_gain, residue, decay_rate, mp_index):
    span = OWNERS * BLOCK
    anywhere = pl.BlockSpec(memory_space=pl.ANY)
    whole = pl.BlockSpec(memory_space=pltpu.VMEM)
    mode_shape = residue.shape[::-1]
    return pl.pallas_call(
        mix_kernel,
        in_specs=[pl.BlockSpec(memory_space=pltpu.SMEM)] + [anywhere] * 5,
        out_specs=[anywhere] + [whole] * 4,
        out_shape=[
            jax.ShapeDtypeStruct((OWNERS, BLOCK, BLOCK), bf16),
            jax.ShapeDtypeStruct((2, OWNERS, 16, BLOCK), f32),
            jax.ShapeDtypeStruct((OWNERS, 8, BLOCK), f32),
            jax.ShapeDtypeStruct((OWNERS, 16, BLOCK), f32),
            jax.ShapeDtypeStruct((2 * MODES, BLOCK), f32),
        ],
        scratch_shapes=[
            pltpu.VMEM(projected.shape, bf16),
            pltpu.VMEM((3, 3, span), f32),
            pltpu.VMEM((1, span), f32),
            pltpu.VMEM(mode_shape, f32),
            pltpu.VMEM(mode_shape, f32),
            pltpu.VMEM((OWNERS, BLOCK, BLOCK), bf16),
            pltpu.SemaphoreType.DMA((4,)),
            pltpu.SemaphoreType.DMA((SIDE, 3)),
            pltpu.SemaphoreType.DMA((SIDE,)),
        ],
        compiler_params=SMALL,
        name="mix",
    )(
        mp_index, in_hbm(projected), in_hbm(short_taps), in_hbm(skip_gain.reshape(1, -1)),
        in_hbm(residue.T), in_hbm(decay_rate.T),
    )


def halo_term(halo, rows, stream):
    at = lax.broadcasted_iota(jnp.int32, (16, BLOCK), 0)
    older = halo[2 * stream : 2 * stream + 1]
    newer = halo[2 * stream + 1 : 2 * stream + 2]
    one = rows[3 + stream : 4 + stream]
    two = rows[6 + stream : 7 + stream]
    return jnp.where(at == 0, one * newer + two * older, jnp.where(at == 1, two * newer, 0.0))


def head_kernel(product_ref, head_ref, halo_ref, rows_ref, out_ref):
    del product_ref
    for g in range(OWNERS):
        halo = halo_ref[g]
        rows = rows_ref[g]
        k_mix = head_ref[0, g] + halo_term(halo, rows, 1)
        v_mix = head_ref[1, g] + halo_term(halo, rows, 2)
        out_ref[g] = (k_mix * v_mix).astype(bf16)


def finish_product(product, head, halo, rows):
    return pl.pallas_call(
        head_kernel,
        grid=(1,),
        in_specs=[
            pl.BlockSpec(memory_space=pl.ANY), full(head.shape), full(halo.shape), full(rows.shape)
        ],
        out_specs=pl.BlockSpec((OWNERS, 16, BLOCK), lambda i: (0, 0, 0)),
        out_shape=jax.ShapeDtypeStruct(product.shape, bf16),
        input_output_aliases={0: 0},
        compiler_params=SMALL,
        name="head",
    )(product, head, halo, rows)


def prepare_kernel(q_ref, product_ref, halo_ref, rows_ref, mix_ref, direct_ref):
    for x in range(SIDE):
        rows = rows_ref[x]
        mix = short_mix(owner_tile(q_ref, 0, x).T.astype(f32), rows, 0)
        mix_ref[x, :16, :] = mix[:16] + halo_term(halo_ref[x], rows, 0)
        mix_ref[x, 16:, :] = mix[16:]
        direct_ref[x] = rows[9:10] * product_ref[x].astype(f32)


def prepare_gate(projected, product, halo, rows):
    tile = lambda n: pl.BlockSpec((4, n, BLOCK), lambda i: (i, 0, 0))
    return pl.pallas_call(
        prepare_kernel,
        grid=(4,),
        in_specs=[
            pl.BlockSpec((1, 512, BLOCK), lambda i: (0, i, 0)), tile(BLOCK), tile(8), tile(16)
        ],
        out_specs=[tile(BLOCK), tile(BLOCK)],
        out_shape=[jax.ShapeDtypeStruct(product.shape, f32)] * 2,
        compiler_params=SMALL,
        name="prepare",
    )(in_hbm(projected), product, halo, rows)


def gate_kernel(mix_ref, direct_ref, long_ref, out_hbm, out_ref, sems):
    copies = [
        pltpu.make_async_copy(
            out_ref.at[pl.ds(512 * y, 512)], out_hbm.at[pl.ds(512 * y, 512)], sems.at[y]
        )
        for y in range(SIDE)
    ]
    for g in range(OWNERS):
        gated = (mix_ref[g] * (long_ref[g].astype(f32) + direct_ref[g])).astype(bf16).T
        for zl, span in enumerate(owner_rows(g)):
            out_ref[span, :] = gated[32 * zl : 32 * zl + 32]
        if g % SIDE == SIDE - 1:
            copies[g // SIDE].start()
    for copy in copies:
        copy.wait()


def apply_gate(mix, direct, long_part):
    shape = (OWNERS * BLOCK, BLOCK)
    return pl.pallas_call(
        gate_kernel,
        in_specs=[pl.BlockSpec(memory_space=pltpu.VMEM)] * 3,
        out_specs=pl.BlockSpec(memory_space=pl.ANY),
        out_shape=jax.ShapeDtypeStruct(shape, bf16),
        scratch_shapes=[pltpu.VMEM(shape, bf16), pltpu.SemaphoreType.DMA((SIDE,))],
        compiler_params=SMALL,
        name="gate",
    )(mix, direct, long_part)


def table_kernel(
    zl_ref, p0_ref, p1_ref, p2_ref, p3_ref, forward_ref,
    spec_ref, step_ref, tail_ref, start_ref, decay_ref,
):
    params = (
        p0_ref[...]
        + pltpu.roll(p1_ref[...], 32, 1)
        + pltpu.roll(p2_ref[...], 64, 1)
        + pltpu.roll(p3_ref[...], 96, 1)
    )
    params = pltpu.roll(params, zl_ref[0] * 32, 1)
    rate = params[:MODES]
    weight = params[MODES:]
    decay_ref[...] = jnp.exp(-float(BLOCK) * rate)
    place = lax.broadcasted_iota(jnp.int32, (BLOCK, BLOCK), 0).astype(f32)
    row = lax.broadcasted_iota(jnp.int32, (8, BLOCK), 0).astype(f32)
    kernel = jnp.zeros((BLOCK, BLOCK), f32)
    for n in range(MODES):
        own = rate[n : n + 1]
        gain = weight[n : n + 1]
        kernel = kernel + gain * jnp.exp(-own * place)
        step_ref[n] = jnp.broadcast_to(jnp.exp(-8.0 * own), (8, BLOCK))
        tail_ref[n] = jnp.exp(-own * (7.0 - row))
        start_ref[n] = gain * jnp.exp(-own * (row + 1.0))
    high, low = split_pair(kernel)
    table = forward_ref[...]
    spec = mm(table, jnp.concatenate([high, high], axis=0)) + mm(table[:, :BLOCK], low)
    spec = spec * (1.0 / BLOCK)
    spec_ref[...] = jnp.concatenate([spec, spec], axis=1)


def make_tables(pieces, forward, zl_index):
    part = jax.ShapeDtypeStruct((MODES, 8, BLOCK), f32)
    return pl.pallas_call(
        table_kernel,
        grid_spec=pltpu.PrefetchScalarGridSpec(
            num_scalar_prefetch=1,
            grid=(1,),
            in_specs=[full((2 * MODES, BLOCK))] * 4 + [full(forward.shape)],
            out_specs=[full((2 * BLOCK, 2 * BLOCK))] + [full(part.shape)] * 3 + [full((MODES, BLOCK))],
        ),
        out_shape=[
            jax.ShapeDtypeStruct((2 * BLOCK, 2 * BLOCK), f32), part, part, part,
            jax.ShapeDtypeStruct((MODES, BLOCK), f32),
        ],
        compiler_params=SMALL,
        name="tables",
    )(zl_index, *pieces, forward)


def state_kernel(x_ref, step_ref, tail_ref, decay_ref, state_ref, run_ref):
    step = step_ref[...]
    tail = tail_ref[...]

    def one_block(b, carry):
        x = x_ref[b].astype(f32)
        state = jnp.zeros((MODES, 8, BLOCK), f32)
        for i in range(BLOCK // 8):
            state = state * step + x[8 * i : 8 * i + 8][None]
        state_ref[b] = jnp.sum(state * tail, axis=1)
        return carry

    lax.fori_loop(0, OWNERS, one_block, 0)
    decay = decay_ref[...]
    for y in range(SIDE):
        run = state_ref[SIDE * y]
        for x in range(1, SIDE):
            run = run * decay + state_ref[SIDE * y + x]
        run_ref[y] = run


def block_states(blocks, step, tail, decay):
    return pl.pallas_call(
        state_kernel,
        out_shape=[
            jax.ShapeDtypeStruct((OWNERS, MODES, BLOCK), f32),
            jax.ShapeDtypeStruct((SIDE, MODES, BLOCK), f32),
        ],
        compiler_params=SMALL,
        name="states",
    )(blocks, step, tail, decay)


def conv_kernel(x_ref, spec_ref, forward_ref, backward_ref, out_ref):
    for pair in range(OWNERS // 2):
        x = jnp.concatenate([x_ref[2 * pair], x_ref[2 * pair + 1]], axis=1)
        turned = mm(forward_ref[...], jnp.concatenate([x, x], axis=0))
        x_re, x_im = turned[:BLOCK], turned[BLOCK:]
        k_re, k_im = spec_ref[:BLOCK, :], spec_ref[BLOCK:, :]
        mixed = jnp.concatenate([x_re * k_re - x_im * k_im, x_re * k_im + x_im * k_re], axis=0)
        high, low = split_pair(mixed)
        both = mm(backward_ref[...], high)
        result = both[:BLOCK] + both[BLOCK:] + mm(backward_ref[:BLOCK, :], low)
        out_ref[2 * pair] = result[:, :BLOCK]
        out_ref[2 * pair + 1] = result[:, BLOCK:]


def convolve_blocks(blocks, spec, forward, backward):
    return pl.pallas_call(
        conv_kernel,
        out_shape=jax.ShapeDtypeStruct(blocks.shape, f32),
        compiler_params=SMALL,
        name="conv",
    )(blocks, spec, forward, backward)


def readout_kernel(
    zl_ref, inner_ref, state_ref, r0_ref, r1_ref, r2_ref, r3_ref, step_ref, start_ref, decay_ref,
    out_ref, runs_ref, enter_ref,
):
    own = zl_ref[0]
    for k, ref in enumerate((r0_ref, r1_ref, r2_ref, r3_ref)):
        runs_ref[(own + k) % SIDE] = ref[...]
    decay = decay_ref[...]
    squared = decay * decay
    run_decay = squared * squared
    state = jnp.zeros((MODES, BLOCK), f32)
    for y in range(SIDE):
        for zl in range(SIDE):

            @pl.when(own == zl)
            def _(state=state, y=y):
                enter_ref[SIDE * y] = state

            state = state * run_decay + runs_ref[zl, y]
        inside = enter_ref[SIDE * y]
        for x in range(1, SIDE):
            inside = inside * decay + state_ref[SIDE * y + x - 1]
            enter_ref[SIDE * y + x] = inside
    step = step_ref[...]

    def one_block(b, carry):
        share = start_ref[...] * enter_ref[b][:, None, :]
        for i in range(BLOCK // 16):
            parts = []
            for half in range(2):
                at = 16 * i + 8 * half
                parts.append(inner_ref[b, at : at + 8, :] + jnp.sum(share, axis=0))
                share = share * step
            out_ref[b, 16 * i : 16 * i + 16, :] = jnp.concatenate(parts, axis=0).astype(bf16)
        return carry

    lax.fori_loop(0, OWNERS, one_block, 0)


def add_states(inner, states, runs, step, start, decay, zl_index):
    return pl.pallas_call(
        readout_kernel,
        grid_spec=pltpu.PrefetchScalarGridSpec(
            num_scalar_prefetch=1,
            grid=(1,),
            in_specs=[full(inner.shape), full(states.shape)]
            + [full((SIDE, MODES, BLOCK))] * 4
            + [full(step.shape)] * 2
            + [full(decay.shape)],
            out_specs=full(inner.shape),
            scratch_shapes=[
                pltpu.VMEM((SIDE, SIDE, MODES, BLOCK), f32),
                pltpu.VMEM((OWNERS, MODES, BLOCK), f32),
            ],
        ),
        out_shape=jax.ShapeDtypeStruct(inner.shape, bf16),
        compiler_params=SMALL,
        name="readout",
    )(zl_index, inner, states, *runs, step, start, decay)


def body(projected, short_taps, skip_gain, residue, decay_rate):
    mp_index = lax.axis_index("mp").astype(jnp.int32).reshape(1)
    zl_index = lax.axis_index("zl").astype(jnp.int32).reshape(1)
    count = SIDE ** 3

    def from_zl(value, k):
        return lax.ppermute(value, "zl", [(zl, (zl - k) % SIDE) for zl in range(SIDE)])

    product, head, halo, rows, params = mix_streams(
        projected, short_taps, skip_gain, residue, decay_rate, mp_index
    )
    halo = lax.ppermute(halo, ("y", "zl", "x"), [(i, i + 1) for i in range(count - 1)])
    pieces = [params] + [from_zl(params, k) for k in range(1, SIDE)]
    product = finish_product(product, head, halo, rows)
    product, *pieces = lax.optimization_barrier((product, *pieces))
    blocks = lax.all_to_all(product, ("y", "x"), split_axis=0, concat_axis=0, tiled=True)
    gate_mix, direct = prepare_gate(projected, product, halo, rows)
    blocks, gate_mix, direct = lax.optimization_barrier((blocks, gate_mix, direct))
    forward, backward = transform_tables()
    spec, step, tail, start, decay = make_tables(pieces, forward, zl_index)
    states, run = block_states(blocks, step, tail, decay)
    runs = [run] + [from_zl(run, k) for k in range(1, SIDE)]
    inner = convolve_blocks(blocks, spec, forward, backward)
    result = add_states(inner, states, runs, step, start, decay, zl_index)
    long_part = lax.all_to_all(result, ("y", "x"), split_axis=0, concat_axis=0, tiled=True)
    return apply_gate(gate_mix, direct, long_part)


def solution(mesh):
    split = Mesh(mesh.devices.reshape(SIDE, SIDE, SIDE, -1), ("y", "zl", "x", "mp"))
    seq = ("y", "zl", "x")
    in_specs = (P(None, "mp", seq), P(), P(), P(seq, None), P(seq, None))
    out_specs = P("mp", seq)
    return jax.shard_map(body, mesh=split, in_specs=in_specs, out_specs=out_specs, check_vma=False)
```

```python
import math

import jax
import jax.numpy as jnp
import ml_dtypes
import numpy as np
from jax import lax
from jax.experimental import pallas as pl
from jax.experimental.pallas import tpu as pltpu
from jax.sharding import Mesh, PartitionSpec as P

BLOCK = 128
MODES = 16
SIDE = 4
OWNERS = SIDE * SIDE
f32 = jnp.float32
bf16 = jnp.bfloat16
SMALL = pltpu.CompilerParams(vmem_limit_bytes=16 << 20)


def split_pair(value):
    high = value.astype(bf16)
    return high, (value - high.astype(f32)).astype(bf16)


def transform_tables():
    steps = np.arange(BLOCK, dtype=np.float64)
    angles = 2.0 * math.pi / BLOCK * np.outer(steps, steps - 0.25)
    table = np.concatenate([np.cos(angles), -np.sin(angles)], axis=1)
    high = table.astype(np.float32).astype(ml_dtypes.bfloat16)
    low = (table - high.astype(np.float64)).astype(np.float32).astype(ml_dtypes.bfloat16)
    forward = np.concatenate([high.T, low.T], axis=1)
    backward = np.concatenate([high, low], axis=0)
    return jnp.asarray(forward), jnp.asarray(backward)


def mm(left, right):
    return lax.dot_general(left, right, (((1,), (0,)), ((), ())), preferred_element_type=f32)


def mm_nt(left, right, precision=None):
    return lax.dot_general(
        left, right, (((1,), (1,)), ((), ())), preferred_element_type=f32, precision=precision
    )


def full(shape):
    return pl.BlockSpec(shape, lambda *_: (0,) * len(shape))


def later(value, steps):
    moved = pltpu.roll(value, steps, 0)
    row = lax.broadcasted_iota(jnp.int32, (8, BLOCK), 0)
    return jnp.concatenate([jnp.where(row < steps, 0.0, moved[:8]), moved[8:]], axis=0)


def short_mix(block, rows, stream):
    return (
        rows[stream : stream + 1] * block
        + rows[3 + stream : 4 + stream] * later(block, 1)
        + rows[6 + stream : 7 + stream] * later(block, 2)
    )


def owner_rows(g):
    first = 512 * (g // SIDE) + 32 * (g % SIDE)
    return [slice(first + 128 * zl, first + 128 * zl + 32) for zl in range(SIDE)]


def owner_tile(x_ref, stream, g):
    return jnp.concatenate([x_ref[stream, span, :] for span in owner_rows(g)], axis=0)


def mix_kernel(
    mp_ref, x_hbm, taps_hbm, skip_hbm, residue_hbm, rate_hbm,
    product_hbm, head_ref, halo_ref, rows_ref, params_ref,
    x_ref, taps_ref, skip_ref, residue_ref, rate_ref, product_ref, small_sems, x_sems, out_sems,
):
    span = OWNERS * BLOCK
    at = pl.multiple_of(mp_ref[0] * span, span)
    small = [
        pltpu.make_async_copy(source, target, small_sems.at[i])
        for i, (source, target) in enumerate(
            (
                (taps_hbm.at[:, :, pl.ds(at, span)], taps_ref),
                (skip_hbm.at[:, pl.ds(at, span)], skip_ref),
                (residue_hbm, residue_ref),
                (rate_hbm, rate_ref),
            )
        )
    ]
    large = [
        [
            pltpu.make_async_copy(
                x_hbm.at[stream, pl.ds(512 * y, 512)],
                x_ref.at[stream, pl.ds(512 * y, 512)],
                x_sems.at[y, stream],
            )
            for stream in range(3)
        ]
        for y in range(SIDE)
    ]
    out = [
        pltpu.make_async_copy(
            product_ref.at[pl.ds(SIDE * y, SIDE)], product_hbm.at[pl.ds(SIDE * y, SIDE)], out_sems.at[y]
        )
        for y in range(SIDE)
    ]
    inner = [large[y][stream] for y in range(SIDE) for stream in (1, 2)]
    outer = [large[y][0] for y in range(SIDE)]
    for copy in small[:2] + inner + outer + small[2:]:
        copy.start()
    lane = lax.broadcasted_iota(jnp.int32, (16, BLOCK), 1) // 32
    small[0].wait()
    small[1].wait()
    for y in range(SIDE):
        table = jnp.concatenate(
            [taps_ref[lag, :, 512 * y : 512 * y + 512] for lag in range(3)]
            + [skip_ref[:, 512 * y : 512 * y + 512], jnp.zeros((6, 4 * BLOCK), f32)],
            axis=0,
        )
        for x in range(SIDE):
            rows = jnp.zeros((16, BLOCK), f32)
            for zl in range(SIDE):
                piece = table[:, zl * BLOCK : (zl + 1) * BLOCK]
                if zl != x:
                    piece = pltpu.roll(piece, (32 * (zl - x)) % BLOCK, 1)
                rows = jnp.where(lane == zl, piece, rows)
            rows_ref[SIDE * y + x] = rows
    for y in range(SIDE):
        large[y][1].wait()
        large[y][2].wait()
        for g in range(SIDE * y, SIDE * y + SIDE):
            rows = rows_ref[g]
            mixes = []
            for stream in (1, 2):
                block = owner_tile(x_ref, stream, g).T.astype(f32)
                halo_ref[g, 2 * stream : 2 * stream + 2, :] = block[BLOCK - 2 :]
                mixes.append(short_mix(block, rows, stream))
                head_ref[stream - 1, g] = mixes[-1][:16]
            product_ref[g] = (mixes[0] * mixes[1]).astype(bf16)
        out[y].start()
    last = lax.broadcasted_iota(jnp.int32, (16, BLOCK), 0) + (BLOCK - 2)
    last = (last == lax.broadcasted_iota(jnp.int32, (16, BLOCK), 1)).astype(bf16)
    for y in range(SIDE):
        large[y][0].wait()
        for g in range(SIDE * y, SIDE * y + SIDE):
            halo_ref[g, 0:2, :] = mm_nt(last, owner_tile(x_ref, 0, g))[0:2]
            halo_ref[g, 6:8, :] = jnp.zeros((2, BLOCK), f32)
    small[2].wait()
    small[3].wait()
    rate = rate_ref[...]
    count = rate.shape[1]
    params_ref[...] = jnp.zeros((2 * MODES, BLOCK), f32)
    params_ref[:MODES, :count] = rate
    params_ref[MODES:, :count] = residue_ref[...] * jnp.sqrt(rate)
    for copy in out:
        copy.wait()


def in_hbm(value):
    return pltpu.with_memory_space_constraint(value, pltpu.HBM)


def mix_streams(projected, short_taps, skip_gain, residue, decay_rate, mp_index):
    span = OWNERS * BLOCK
    anywhere = pl.BlockSpec(memory_space=pl.ANY)
    whole = pl.BlockSpec(memory_space=pltpu.VMEM)
    mode_shape = residue.shape[::-1]
    return pl.pallas_call(
        mix_kernel,
        in_specs=[pl.BlockSpec(memory_space=pltpu.SMEM)] + [anywhere] * 5,
        out_specs=[anywhere] + [whole] * 4,
        out_shape=[
            jax.ShapeDtypeStruct((OWNERS, BLOCK, BLOCK), bf16),
            jax.ShapeDtypeStruct((2, OWNERS, 16, BLOCK), f32),
            jax.ShapeDtypeStruct((OWNERS, 8, BLOCK), f32),
            jax.ShapeDtypeStruct((OWNERS, 16, BLOCK), f32),
            jax.ShapeDtypeStruct((2 * MODES, BLOCK), f32),
        ],
        scratch_shapes=[
            pltpu.VMEM(projected.shape, bf16),
            pltpu.VMEM((3, 3, span), f32),
            pltpu.VMEM((1, span), f32),
            pltpu.VMEM(mode_shape, f32),
            pltpu.VMEM(mode_shape, f32),
            pltpu.VMEM((OWNERS, BLOCK, BLOCK), bf16),
            pltpu.SemaphoreType.DMA((4,)),
            pltpu.SemaphoreType.DMA((SIDE, 3)),
            pltpu.SemaphoreType.DMA((SIDE,)),
        ],
        compiler_params=SMALL,
        name="mix",
    )(
        mp_index, in_hbm(projected), in_hbm(short_taps), in_hbm(skip_gain.reshape(1, -1)),
        in_hbm(residue.T), in_hbm(decay_rate.T),
    )


def halo_term(halo, rows, stream):
    at = lax.broadcasted_iota(jnp.int32, (16, BLOCK), 0)
    older = halo[2 * stream : 2 * stream + 1]
    newer = halo[2 * stream + 1 : 2 * stream + 2]
    one = rows[3 + stream : 4 + stream]
    two = rows[6 + stream : 7 + stream]
    return jnp.where(at == 0, one * newer + two * older, jnp.where(at == 1, two * newer, 0.0))


def head_kernel(product_ref, head_ref, halo_ref, rows_ref, out_ref):
    del product_ref
    for g in range(OWNERS):
        halo = halo_ref[g]
        rows = rows_ref[g]
        k_mix = head_ref[0, g] + halo_term(halo, rows, 1)
        v_mix = head_ref[1, g] + halo_term(halo, rows, 2)
        out_ref[g] = (k_mix * v_mix).astype(bf16)


def finish_product(product, head, halo, rows):
    return pl.pallas_call(
        head_kernel,
        grid=(1,),
        in_specs=[
            pl.BlockSpec(memory_space=pl.ANY), full(head.shape), full(halo.shape), full(rows.shape)
        ],
        out_specs=pl.BlockSpec((OWNERS, 16, BLOCK), lambda i: (0, 0, 0)),
        out_shape=jax.ShapeDtypeStruct(product.shape, bf16),
        input_output_aliases={0: 0},
        compiler_params=SMALL,
        name="head",
    )(product, head, halo, rows)


def prepare_kernel(q_ref, product_ref, halo_ref, rows_ref, mix_ref, direct_ref):
    for x in range(SIDE):
        rows = rows_ref[x]
        mix = short_mix(owner_tile(q_ref, 0, x).T.astype(f32), rows, 0)
        mix_ref[x, :16, :] = mix[:16] + halo_term(halo_ref[x], rows, 0)
        mix_ref[x, 16:, :] = mix[16:]
        direct_ref[x] = rows[9:10] * product_ref[x].astype(f32)


def prepare_gate(projected, product, halo, rows):
    tile = lambda n: pl.BlockSpec((4, n, BLOCK), lambda i: (i, 0, 0))
    return pl.pallas_call(
        prepare_kernel,
        grid=(4,),
        in_specs=[
            pl.BlockSpec((1, 512, BLOCK), lambda i: (0, i, 0)), tile(BLOCK), tile(8), tile(16)
        ],
        out_specs=[tile(BLOCK), tile(BLOCK)],
        out_shape=[jax.ShapeDtypeStruct(product.shape, f32)] * 2,
        compiler_params=SMALL,
        name="prepare",
    )(in_hbm(projected), product, halo, rows)


def gate_kernel(mix_ref, direct_ref, long_ref, out_hbm, out_ref, sems):
    copies = [
        pltpu.make_async_copy(
            out_ref.at[pl.ds(512 * y, 512)], out_hbm.at[pl.ds(512 * y, 512)], sems.at[y]
        )
        for y in range(SIDE)
    ]
    for g in range(OWNERS):
        gated = (mix_ref[g] * (long_ref[g].astype(f32) + direct_ref[g])).astype(bf16).T
        for zl, span in enumerate(owner_rows(g)):
            out_ref[span, :] = gated[32 * zl : 32 * zl + 32]
        if g % SIDE == SIDE - 1:
            copies[g // SIDE].start()
    for copy in copies:
        copy.wait()


def apply_gate(mix, direct, long_part):
    shape = (OWNERS * BLOCK, BLOCK)
    return pl.pallas_call(
        gate_kernel,
        in_specs=[pl.BlockSpec(memory_space=pltpu.VMEM)] * 3,
        out_specs=pl.BlockSpec(memory_space=pl.ANY),
        out_shape=jax.ShapeDtypeStruct(shape, bf16),
        scratch_shapes=[pltpu.VMEM(shape, bf16), pltpu.SemaphoreType.DMA((SIDE,))],
        compiler_params=SMALL,
        name="gate",
    )(mix, direct, long_part)


def table_kernel(
    zl_ref, p0_ref, p1_ref, p2_ref, p3_ref, forward_ref,
    spec_ref, step_ref, tail_ref, start_ref, decay_ref,
):
    params = (
        p0_ref[...]
        + pltpu.roll(p1_ref[...], 32, 1)
        + pltpu.roll(p2_ref[...], 64, 1)
        + pltpu.roll(p3_ref[...], 96, 1)
    )
    params = pltpu.roll(params, zl_ref[0] * 32, 1)
    rate = params[:MODES]
    weight = params[MODES:]
    decay_ref[...] = jnp.exp(-float(BLOCK) * rate)
    place = lax.broadcasted_iota(jnp.int32, (BLOCK, BLOCK), 0).astype(f32)
    row = lax.broadcasted_iota(jnp.int32, (8, BLOCK), 0).astype(f32)
    kernel = jnp.zeros((BLOCK, BLOCK), f32)
    for n in range(MODES):
        own = rate[n : n + 1]
        gain = weight[n : n + 1]
        kernel = kernel + gain * jnp.exp(-own * place)
        step_ref[n] = jnp.broadcast_to(jnp.exp(-8.0 * own), (8, BLOCK))
        tail_ref[n] = jnp.exp(-own * (7.0 - row))
        start_ref[n] = gain * jnp.exp(-own * (row + 1.0))
    high, low = split_pair(kernel)
    table = forward_ref[...]
    spec = mm(table, jnp.concatenate([high, high], axis=0)) + mm(table[:, :BLOCK], low)
    spec = spec * (1.0 / BLOCK)
    spec_ref[...] = jnp.concatenate([spec, spec], axis=1)


def make_tables(pieces, forward, zl_index):
    part = jax.ShapeDtypeStruct((MODES, 8, BLOCK), f32)
    return pl.pallas_call(
        table_kernel,
        grid_spec=pltpu.PrefetchScalarGridSpec(
            num_scalar_prefetch=1,
            grid=(1,),
            in_specs=[full((2 * MODES, BLOCK))] * 4 + [full(forward.shape)],
            out_specs=[full((2 * BLOCK, 2 * BLOCK))] + [full(part.shape)] * 3 + [full((MODES, BLOCK))],
        ),
        out_shape=[
            jax.ShapeDtypeStruct((2 * BLOCK, 2 * BLOCK), f32), part, part, part,
            jax.ShapeDtypeStruct((MODES, BLOCK), f32),
        ],
        compiler_params=SMALL,
        name="tables",
    )(zl_index, *pieces, forward)


def state_kernel(x_ref, step_ref, tail_ref, decay_ref, state_ref, run_ref):
    step = step_ref[...]
    tail = tail_ref[...]

    def one_block(b, carry):
        x = x_ref[b].astype(f32)
        state = jnp.zeros((MODES, 8, BLOCK), f32)
        for i in range(BLOCK // 8):
            state = state * step + x[8 * i : 8 * i + 8][None]
        state_ref[b] = jnp.sum(state * tail, axis=1)
        return carry

    lax.fori_loop(0, OWNERS, one_block, 0)
    decay = decay_ref[...]
    for y in range(SIDE):
        run = state_ref[SIDE * y]
        for x in range(1, SIDE):
            run = run * decay + state_ref[SIDE * y + x]
        run_ref[y] = run


def block_states(blocks, step, tail, decay):
    return pl.pallas_call(
        state_kernel,
        out_shape=[
            jax.ShapeDtypeStruct((OWNERS, MODES, BLOCK), f32),
            jax.ShapeDtypeStruct((SIDE, MODES, BLOCK), f32),
        ],
        compiler_params=SMALL,
        name="states",
    )(blocks, step, tail, decay)


def conv_kernel(x_ref, spec_ref, forward_ref, backward_ref, out_ref):
    for pair in range(OWNERS // 2):
        x = jnp.concatenate([x_ref[2 * pair], x_ref[2 * pair + 1]], axis=1)
        turned = mm(forward_ref[...], jnp.concatenate([x, x], axis=0))
        x_re, x_im = turned[:BLOCK], turned[BLOCK:]
        k_re, k_im = spec_ref[:BLOCK, :], spec_ref[BLOCK:, :]
        mixed = jnp.concatenate([x_re * k_re - x_im * k_im, x_re * k_im + x_im * k_re], axis=0)
        high, low = split_pair(mixed)
        both = mm(backward_ref[...], high)
        result = both[:BLOCK] + both[BLOCK:] + mm(backward_ref[:BLOCK, :], low)
        out_ref[2 * pair] = result[:, :BLOCK]
        out_ref[2 * pair + 1] = result[:, BLOCK:]


def convolve_blocks(blocks, spec, forward, backward):
    return pl.pallas_call(
        conv_kernel,
        out_shape=jax.ShapeDtypeStruct(blocks.shape, f32),
        compiler_params=SMALL,
        name="conv",
    )(blocks, spec, forward, backward)


def readout_kernel(
    zl_ref, inner_ref, state_ref, r0_ref, r1_ref, r2_ref, r3_ref, step_ref, start_ref, decay_ref,
    out_ref, runs_ref, enter_ref,
):
    own = zl_ref[0]
    for k, ref in enumerate((r0_ref, r1_ref, r2_ref, r3_ref)):
        runs_ref[(own + k) % SIDE] = ref[...]
    decay = decay_ref[...]
    squared = decay * decay
    run_decay = squared * squared
    state = jnp.zeros((MODES, BLOCK), f32)
    for y in range(SIDE):
        for zl in range(SIDE):

            @pl.when(own == zl)
            def _(state=state, y=y):
                enter_ref[SIDE * y] = state

            state = state * run_decay + runs_ref[zl, y]
        inside = enter_ref[SIDE * y]
        for x in range(1, SIDE):
            inside = inside * decay + state_ref[SIDE * y + x - 1]
            enter_ref[SIDE * y + x] = inside
    step = step_ref[...]

    def one_block(b, carry):
        share = start_ref[...] * enter_ref[b][:, None, :]
        for i in range(BLOCK // 16):
            parts = []
            for half in range(2):
                at = 16 * i + 8 * half
                parts.append(inner_ref[b, at : at + 8, :] + jnp.sum(share, axis=0))
                share = share * step
            out_ref[b, 16 * i : 16 * i + 16, :] = jnp.concatenate(parts, axis=0).astype(bf16)
        return carry

    lax.fori_loop(0, OWNERS, one_block, 0)


def add_states(inner, states, runs, step, start, decay, zl_index):
    return pl.pallas_call(
        readout_kernel,
        grid_spec=pltpu.PrefetchScalarGridSpec(
            num_scalar_prefetch=1,
            grid=(1,),
            in_specs=[full(inner.shape), full(states.shape)]
            + [full((SIDE, MODES, BLOCK))] * 4
            + [full(step.shape)] * 2
            + [full(decay.shape)],
            out_specs=full(inner.shape),
            scratch_shapes=[
                pltpu.VMEM((SIDE, SIDE, MODES, BLOCK), f32),
                pltpu.VMEM((OWNERS, MODES, BLOCK), f32),
            ],
        ),
        out_shape=jax.ShapeDtypeStruct(inner.shape, bf16),
        compiler_params=SMALL,
        name="readout",
    )(zl_index, inner, states, *runs, step, start, decay)


def body(projected, short_taps, skip_gain, residue, decay_rate):
    mp_index = lax.axis_index("mp").astype(jnp.int32).reshape(1)
    zl_index = lax.axis_index("zl").astype(jnp.int32).reshape(1)
    count = SIDE ** 3

    def from_zl(value, k):
        return lax.ppermute(value, "zl", [(zl, (zl - k) % SIDE) for zl in range(SIDE)])

    product, head, halo, rows, params = mix_streams(
        projected, short_taps, skip_gain, residue, decay_rate, mp_index
    )
    halo = lax.ppermute(halo, ("y", "zl", "x"), [(i, i + 1) for i in range(count - 1)])
    pieces = [params] + [from_zl(params, k) for k in range(1, SIDE)]
    product = finish_product(product, head, halo, rows)
    product, pieces[1] = lax.optimization_barrier((product, pieces[1]))
    blocks = lax.all_to_all(product, ("y", "x"), split_axis=0, concat_axis=0, tiled=True)
    gate_mix, direct = prepare_gate(projected, product, halo, rows)
    blocks, gate_mix, direct = lax.optimization_barrier((blocks, gate_mix, direct))
    forward, backward = transform_tables()
    spec, step, tail, start, decay = make_tables(pieces, forward, zl_index)
    states, run = block_states(blocks, step, tail, decay)
    runs = [run] + [from_zl(run, k) for k in range(1, SIDE)]
    inner = convolve_blocks(blocks, spec, forward, backward)
    result = add_states(inner, states, runs, step, start, decay, zl_index)
    long_part = lax.all_to_all(result, ("y", "x"), split_axis=0, concat_axis=0, tiled=True)
    return apply_gate(gate_mix, direct, long_part)


def solution(mesh):
    split = Mesh(mesh.devices.reshape(SIDE, SIDE, SIDE, -1), ("y", "zl", "x", "mp"))
    seq = ("y", "zl", "x")
    in_specs = (P(None, "mp", seq), P(), P(), P(seq, None), P(seq, None))
    out_specs = P("mp", seq)
    return jax.shard_map(body, mesh=split, in_specs=in_specs, out_specs=out_specs, check_vma=False)
```

```python
import math

import jax
import jax.numpy as jnp
import ml_dtypes
import numpy as np
from jax import lax
from jax.experimental import pallas as pl
from jax.experimental.pallas import tpu as pltpu
from jax.sharding import Mesh, PartitionSpec as P

BLOCK = 128
MODES = 16
SIDE = 4
OWNERS = SIDE * SIDE
f32 = jnp.float32
bf16 = jnp.bfloat16
SMALL = pltpu.CompilerParams(vmem_limit_bytes=16 << 20)


def split_pair(value):
    high = value.astype(bf16)
    return high, (value - high.astype(f32)).astype(bf16)


def transform_tables():
    steps = np.arange(BLOCK, dtype=np.float64)
    angles = 2.0 * math.pi / BLOCK * np.outer(steps, steps - 0.25)
    table = np.concatenate([np.cos(angles), -np.sin(angles)], axis=1)
    high = table.astype(np.float32).astype(ml_dtypes.bfloat16)
    low = (table - high.astype(np.float64)).astype(np.float32).astype(ml_dtypes.bfloat16)
    forward = np.concatenate([high.T, low.T], axis=1)
    backward = np.concatenate([high, low], axis=0)
    return jnp.asarray(forward), jnp.asarray(backward)


def mm(left, right):
    return lax.dot_general(left, right, (((1,), (0,)), ((), ())), preferred_element_type=f32)


def mm_nt(left, right, precision=None):
    return lax.dot_general(
        left, right, (((1,), (1,)), ((), ())), preferred_element_type=f32, precision=precision
    )


def full(shape):
    return pl.BlockSpec(shape, lambda *_: (0,) * len(shape))


def later(value, steps):
    moved = pltpu.roll(value, steps, 0)
    row = lax.broadcasted_iota(jnp.int32, (8, BLOCK), 0)
    return jnp.concatenate([jnp.where(row < steps, 0.0, moved[:8]), moved[8:]], axis=0)


def short_mix(block, rows, stream):
    return (
        rows[stream : stream + 1] * block
        + rows[3 + stream : 4 + stream] * later(block, 1)
        + rows[6 + stream : 7 + stream] * later(block, 2)
    )


def owner_rows(g):
    first = 512 * (g // SIDE) + 32 * (g % SIDE)
    return [slice(first + 128 * zl, first + 128 * zl + 32) for zl in range(SIDE)]


def owner_tile(x_ref, stream, g):
    return jnp.concatenate([x_ref[stream, span, :] for span in owner_rows(g)], axis=0)


def mix_kernel(
    mp_ref, x_hbm, taps_hbm, skip_hbm, residue_hbm, rate_hbm,
    product_hbm, head_ref, halo_ref, rows_ref, params_ref,
    x_ref, taps_ref, skip_ref, residue_ref, rate_ref, product_ref, small_sems, x_sems, out_sems,
):
    span = OWNERS * BLOCK
    at = pl.multiple_of(mp_ref[0] * span, span)
    small = [
        pltpu.make_async_copy(source, target, small_sems.at[i])
        for i, (source, target) in enumerate(
            (
                (taps_hbm.at[:, :, pl.ds(at, span)], taps_ref),
                (skip_hbm.at[:, pl.ds(at, span)], skip_ref),
                (residue_hbm, residue_ref),
                (rate_hbm, rate_ref),
            )
        )
    ]
    large = [
        [
            pltpu.make_async_copy(
                x_hbm.at[stream, pl.ds(512 * y, 512)],
                x_ref.at[stream, pl.ds(512 * y, 512)],
                x_sems.at[y, stream],
            )
            for stream in range(3)
        ]
        for y in range(SIDE)
    ]
    out = [
        pltpu.make_async_copy(
            product_ref.at[pl.ds(SIDE * y, SIDE)], product_hbm.at[pl.ds(SIDE * y, SIDE)], out_sems.at[y]
        )
        for y in range(SIDE)
    ]
    inner = [large[y][stream] for y in range(SIDE) for stream in (1, 2)]
    outer = [large[y][0] for y in range(SIDE)]
    for copy in small[:2] + inner + outer + small[2:]:
        copy.start()
    lane = lax.broadcasted_iota(jnp.int32, (16, BLOCK), 1) // 32
    small[0].wait()
    small[1].wait()
    for y in range(SIDE):
        table = jnp.concatenate(
            [taps_ref[lag, :, 512 * y : 512 * y + 512] for lag in range(3)]
            + [skip_ref[:, 512 * y : 512 * y + 512], jnp.zeros((6, 4 * BLOCK), f32)],
            axis=0,
        )
        for x in range(SIDE):
            rows = jnp.zeros((16, BLOCK), f32)
            for zl in range(SIDE):
                piece = table[:, zl * BLOCK : (zl + 1) * BLOCK]
                if zl != x:
                    piece = pltpu.roll(piece, (32 * (zl - x)) % BLOCK, 1)
                rows = jnp.where(lane == zl, piece, rows)
            rows_ref[SIDE * y + x] = rows
    for y in range(SIDE):
        large[y][1].wait()
        large[y][2].wait()
        for g in range(SIDE * y, SIDE * y + SIDE):
            rows = rows_ref[g]
            mixes = []
            for stream in (1, 2):
                block = owner_tile(x_ref, stream, g).T.astype(f32)
                halo_ref[g, 2 * stream : 2 * stream + 2, :] = block[BLOCK - 2 :]
                mixes.append(short_mix(block, rows, stream))
                head_ref[stream - 1, g] = mixes[-1][:16]
            product_ref[g] = (mixes[0] * mixes[1]).astype(bf16)
        out[y].start()
    last = lax.broadcasted_iota(jnp.int32, (16, BLOCK), 0) + (BLOCK - 2)
    last = (last == lax.broadcasted_iota(jnp.int32, (16, BLOCK), 1)).astype(bf16)
    for y in range(SIDE):
        large[y][0].wait()
        for g in range(SIDE * y, SIDE * y + SIDE):
            halo_ref[g, 0:2, :] = mm_nt(last, owner_tile(x_ref, 0, g))[0:2]
            halo_ref[g, 6:8, :] = jnp.zeros((2, BLOCK), f32)
    small[2].wait()
    small[3].wait()
    rate = rate_ref[...]
    count = rate.shape[1]
    params_ref[...] = jnp.zeros((2 * MODES, BLOCK), f32)
    params_ref[:MODES, :count] = rate
    params_ref[MODES:, :count] = residue_ref[...] * jnp.sqrt(rate)
    for copy in out:
        copy.wait()


def in_hbm(value):
    return pltpu.with_memory_space_constraint(value, pltpu.HBM)


def mix_streams(projected, short_taps, skip_gain, residue, decay_rate, mp_index):
    span = OWNERS * BLOCK
    anywhere = pl.BlockSpec(memory_space=pl.ANY)
    whole = pl.BlockSpec(memory_space=pltpu.VMEM)
    mode_shape = residue.shape[::-1]
    return pl.pallas_call(
        mix_kernel,
        in_specs=[pl.BlockSpec(memory_space=pltpu.SMEM)] + [anywhere] * 5,
        out_specs=[anywhere] + [whole] * 4,
        out_shape=[
            jax.ShapeDtypeStruct((OWNERS, BLOCK, BLOCK), bf16),
            jax.ShapeDtypeStruct((2, OWNERS, 16, BLOCK), f32),
            jax.ShapeDtypeStruct((OWNERS, 8, BLOCK), f32),
            jax.ShapeDtypeStruct((OWNERS, 16, BLOCK), f32),
            jax.ShapeDtypeStruct((2 * MODES, BLOCK), f32),
        ],
        scratch_shapes=[
            pltpu.VMEM(projected.shape, bf16),
            pltpu.VMEM((3, 3, span), f32),
            pltpu.VMEM((1, span), f32),
            pltpu.VMEM(mode_shape, f32),
            pltpu.VMEM(mode_shape, f32),
            pltpu.VMEM((OWNERS, BLOCK, BLOCK), bf16),
            pltpu.SemaphoreType.DMA((4,)),
            pltpu.SemaphoreType.DMA((SIDE, 3)),
            pltpu.SemaphoreType.DMA((SIDE,)),
        ],
        compiler_params=SMALL,
        name="mix",
    )(
        mp_index, in_hbm(projected), in_hbm(short_taps), in_hbm(skip_gain.reshape(1, -1)),
        in_hbm(residue.T), in_hbm(decay_rate.T),
    )


def halo_term(halo, rows, stream):
    at = lax.broadcasted_iota(jnp.int32, (16, BLOCK), 0)
    older = halo[2 * stream : 2 * stream + 1]
    newer = halo[2 * stream + 1 : 2 * stream + 2]
    one = rows[3 + stream : 4 + stream]
    two = rows[6 + stream : 7 + stream]
    return jnp.where(at == 0, one * newer + two * older, jnp.where(at == 1, two * newer, 0.0))


def head_kernel(product_ref, head_ref, halo_ref, rows_ref, out_ref):
    del product_ref
    for g in range(OWNERS):
        halo = halo_ref[g]
        rows = rows_ref[g]
        k_mix = head_ref[0, g] + halo_term(halo, rows, 1)
        v_mix = head_ref[1, g] + halo_term(halo, rows, 2)
        out_ref[g] = (k_mix * v_mix).astype(bf16)


def finish_product(product, head, halo, rows):
    return pl.pallas_call(
        head_kernel,
        grid=(1,),
        in_specs=[
            pl.BlockSpec(memory_space=pl.ANY), full(head.shape), full(halo.shape), full(rows.shape)
        ],
        out_specs=pl.BlockSpec((OWNERS, 16, BLOCK), lambda i: (0, 0, 0)),
        out_shape=jax.ShapeDtypeStruct(product.shape, bf16),
        input_output_aliases={0: 0},
        compiler_params=SMALL,
        name="head",
    )(product, head, halo, rows)


def prepare_kernel(q_ref, product_ref, halo_ref, rows_ref, mix_ref, direct_ref):
    for x in range(SIDE):
        rows = rows_ref[x]
        mix = short_mix(owner_tile(q_ref, 0, x).T.astype(f32), rows, 0)
        mix_ref[x, :16, :] = mix[:16] + halo_term(halo_ref[x], rows, 0)
        mix_ref[x, 16:, :] = mix[16:]
        direct_ref[x] = rows[9:10] * product_ref[x].astype(f32)


def prepare_gate(projected, product, halo, rows):
    tile = lambda n: pl.BlockSpec((4, n, BLOCK), lambda i: (i, 0, 0))
    return pl.pallas_call(
        prepare_kernel,
        grid=(4,),
        in_specs=[
            pl.BlockSpec((1, 512, BLOCK), lambda i: (0, i, 0)), tile(BLOCK), tile(8), tile(16)
        ],
        out_specs=[tile(BLOCK), tile(BLOCK)],
        out_shape=[jax.ShapeDtypeStruct(product.shape, f32)] * 2,
        compiler_params=SMALL,
        name="prepare",
    )(in_hbm(projected), product, halo, rows)


def gate_kernel(mix_ref, direct_ref, long_ref, out_hbm, out_ref, sems):
    copies = [
        pltpu.make_async_copy(
            out_ref.at[pl.ds(512 * y, 512)], out_hbm.at[pl.ds(512 * y, 512)], sems.at[y]
        )
        for y in range(SIDE)
    ]
    for g in range(OWNERS):
        gated = (mix_ref[g] * (long_ref[g].astype(f32) + direct_ref[g])).astype(bf16).T
        for zl, span in enumerate(owner_rows(g)):
            out_ref[span, :] = gated[32 * zl : 32 * zl + 32]
        if g % SIDE == SIDE - 1:
            copies[g // SIDE].start()
    for copy in copies:
        copy.wait()


def apply_gate(mix, direct, long_part):
    shape = (OWNERS * BLOCK, BLOCK)
    return pl.pallas_call(
        gate_kernel,
        in_specs=[pl.BlockSpec(memory_space=pltpu.VMEM)] * 3,
        out_specs=pl.BlockSpec(memory_space=pl.ANY),
        out_shape=jax.ShapeDtypeStruct(shape, bf16),
        scratch_shapes=[pltpu.VMEM(shape, bf16), pltpu.SemaphoreType.DMA((SIDE,))],
        compiler_params=SMALL,
        name="gate",
    )(mix, direct, long_part)


def table_kernel(
    zl_ref, p0_ref, p1_ref, p2_ref, p3_ref, forward_ref,
    spec_ref, step_ref, tail_ref, start_ref, decay_ref,
):
    params = (
        p0_ref[...]
        + pltpu.roll(p1_ref[...], 32, 1)
        + pltpu.roll(p2_ref[...], 64, 1)
        + pltpu.roll(p3_ref[...], 96, 1)
    )
    params = pltpu.roll(params, zl_ref[0] * 32, 1)
    rate = params[:MODES]
    weight = params[MODES:]
    decay_ref[...] = jnp.exp(-float(BLOCK) * rate)
    place = lax.broadcasted_iota(jnp.int32, (BLOCK, BLOCK), 0).astype(f32)
    row = lax.broadcasted_iota(jnp.int32, (8, BLOCK), 0).astype(f32)
    kernel = jnp.zeros((BLOCK, BLOCK), f32)
    for n in range(MODES):
        own = rate[n : n + 1]
        gain = weight[n : n + 1]
        kernel = kernel + gain * jnp.exp(-own * place)
        step_ref[n] = jnp.broadcast_to(jnp.exp(-8.0 * own), (8, BLOCK))
        tail_ref[n] = jnp.exp(-own * (7.0 - row))
        start_ref[n] = gain * jnp.exp(-own * (row + 1.0))
    high, low = split_pair(kernel)
    table = forward_ref[...]
    spec = mm(table, jnp.concatenate([high, high], axis=0)) + mm(table[:, :BLOCK], low)
    spec = spec * (1.0 / BLOCK)
    spec_ref[...] = jnp.concatenate([spec, spec], axis=1)


def make_tables(pieces, forward, zl_index):
    part = jax.ShapeDtypeStruct((MODES, 8, BLOCK), f32)
    return pl.pallas_call(
        table_kernel,
        grid_spec=pltpu.PrefetchScalarGridSpec(
            num_scalar_prefetch=1,
            grid=(1,),
            in_specs=[full((2 * MODES, BLOCK))] * 4 + [full(forward.shape)],
            out_specs=[full((2 * BLOCK, 2 * BLOCK))] + [full(part.shape)] * 3 + [full((MODES, BLOCK))],
        ),
        out_shape=[
            jax.ShapeDtypeStruct((2 * BLOCK, 2 * BLOCK), f32), part, part, part,
            jax.ShapeDtypeStruct((MODES, BLOCK), f32),
        ],
        compiler_params=SMALL,
        name="tables",
    )(zl_index, *pieces, forward)


def state_kernel(x_ref, step_ref, tail_ref, decay_ref, state_ref, run_ref):
    step = step_ref[...]
    tail = tail_ref[...]

    def one_block(b, carry):
        x = x_ref[b].astype(f32)
        state = jnp.zeros((MODES, 8, BLOCK), f32)
        for i in range(BLOCK // 8):
            state = state * step + x[8 * i : 8 * i + 8][None]
        state_ref[b] = jnp.sum(state * tail, axis=1)
        return carry

    lax.fori_loop(0, OWNERS, one_block, 0)
    decay = decay_ref[...]
    for y in range(SIDE):
        run = state_ref[SIDE * y]
        for x in range(1, SIDE):
            run = run * decay + state_ref[SIDE * y + x]
        run_ref[y] = run


def block_states(blocks, step, tail, decay):
    return pl.pallas_call(
        state_kernel,
        out_shape=[
            jax.ShapeDtypeStruct((OWNERS, MODES, BLOCK), f32),
            jax.ShapeDtypeStruct((SIDE, MODES, BLOCK), f32),
        ],
        compiler_params=SMALL,
        name="states",
    )(blocks, step, tail, decay)


def conv_kernel(x_ref, spec_ref, forward_ref, backward_ref, out_ref):
    for pair in range(OWNERS // 2):
        x = jnp.concatenate([x_ref[2 * pair], x_ref[2 * pair + 1]], axis=1)
        turned = mm(forward_ref[...], jnp.concatenate([x, x], axis=0))
        x_re, x_im = turned[:BLOCK], turned[BLOCK:]
        k_re, k_im = spec_ref[:BLOCK, :], spec_ref[BLOCK:, :]
        mixed = jnp.concatenate([x_re * k_re - x_im * k_im, x_re * k_im + x_im * k_re], axis=0)
        high, low = split_pair(mixed)
        both = mm(backward_ref[...], high)
        result = both[:BLOCK] + both[BLOCK:] + mm(backward_ref[:BLOCK, :], low)
        out_ref[2 * pair] = result[:, :BLOCK]
        out_ref[2 * pair + 1] = result[:, BLOCK:]


def convolve_blocks(blocks, spec, forward, backward):
    return pl.pallas_call(
        conv_kernel,
        out_shape=jax.ShapeDtypeStruct(blocks.shape, f32),
        compiler_params=SMALL,
        name="conv",
    )(blocks, spec, forward, backward)


def readout_kernel(
    zl_ref, inner_ref, state_ref, r0_ref, r1_ref, r2_ref, r3_ref, step_ref, start_ref, decay_ref,
    out_ref, runs_ref, enter_ref,
):
    own = zl_ref[0]
    for k, ref in enumerate((r0_ref, r1_ref, r2_ref, r3_ref)):
        runs_ref[(own + k) % SIDE] = ref[...]
    decay = decay_ref[...]
    squared = decay * decay
    run_decay = squared * squared
    state = jnp.zeros((MODES, BLOCK), f32)
    for y in range(SIDE):
        for zl in range(SIDE):

            @pl.when(own == zl)
            def _(state=state, y=y):
                enter_ref[SIDE * y] = state

            state = state * run_decay + runs_ref[zl, y]
        inside = enter_ref[SIDE * y]
        for x in range(1, SIDE):
            inside = inside * decay + state_ref[SIDE * y + x - 1]
            enter_ref[SIDE * y + x] = inside
    step = step_ref[...]

    def one_block(b, carry):
        share = start_ref[...] * enter_ref[b][:, None, :]
        for i in range(BLOCK // 16):
            parts = []
            for half in range(2):
                at = 16 * i + 8 * half
                parts.append(inner_ref[b, at : at + 8, :] + jnp.sum(share, axis=0))
                share = share * step
            out_ref[b, 16 * i : 16 * i + 16, :] = jnp.concatenate(parts, axis=0).astype(bf16)
        return carry

    lax.fori_loop(0, OWNERS, one_block, 0)


def add_states(inner, states, runs, step, start, decay, zl_index):
    return pl.pallas_call(
        readout_kernel,
        grid_spec=pltpu.PrefetchScalarGridSpec(
            num_scalar_prefetch=1,
            grid=(1,),
            in_specs=[full(inner.shape), full(states.shape)]
            + [full((SIDE, MODES, BLOCK))] * 4
            + [full(step.shape)] * 2
            + [full(decay.shape)],
            out_specs=full(inner.shape),
            scratch_shapes=[
                pltpu.VMEM((SIDE, SIDE, MODES, BLOCK), f32),
                pltpu.VMEM((OWNERS, MODES, BLOCK), f32),
            ],
        ),
        out_shape=jax.ShapeDtypeStruct(inner.shape, bf16),
        compiler_params=SMALL,
        name="readout",
    )(zl_index, inner, states, *runs, step, start, decay)


def body(projected, short_taps, skip_gain, residue, decay_rate):
    mp_index = lax.axis_index("mp").astype(jnp.int32).reshape(1)
    zl_index = lax.axis_index("zl").astype(jnp.int32).reshape(1)
    count = SIDE ** 3

    def from_zl(value, k):
        return lax.ppermute(value, "zl", [(zl, (zl - k) % SIDE) for zl in range(SIDE)])

    product, head, halo, rows, params = mix_streams(
        projected, short_taps, skip_gain, residue, decay_rate, mp_index
    )
    halo = lax.ppermute(halo, ("y", "zl", "x"), [(i, i + 1) for i in range(count - 1)])
    pieces = [params] + [from_zl(params, k) for k in range(1, SIDE)]
    product = finish_product(product, head, halo, rows)
    product, pieces[3] = lax.optimization_barrier((product, pieces[3]))
    blocks = lax.all_to_all(product, ("y", "x"), split_axis=0, concat_axis=0, tiled=True)
    gate_mix, direct = prepare_gate(projected, product, halo, rows)
    blocks, gate_mix, direct = lax.optimization_barrier((blocks, gate_mix, direct))
    forward, backward = transform_tables()
    spec, step, tail, start, decay = make_tables(pieces, forward, zl_index)
    states, run = block_states(blocks, step, tail, decay)
    runs = [run] + [from_zl(run, k) for k in range(1, SIDE)]
    inner = convolve_blocks(blocks, spec, forward, backward)
    result = add_states(inner, states, runs, step, start, decay, zl_index)
    long_part = lax.all_to_all(result, ("y", "x"), split_axis=0, concat_axis=0, tiled=True)
    return apply_gate(gate_mix, direct, long_part)


def solution(mesh):
    split = Mesh(mesh.devices.reshape(SIDE, SIDE, SIDE, -1), ("y", "zl", "x", "mp"))
    seq = ("y", "zl", "x")
    in_specs = (P(None, "mp", seq), P(), P(), P(seq, None), P(seq, None))
    out_specs = P("mp", seq)
    return jax.shard_map(body, mesh=split, in_specs=in_specs, out_specs=out_specs, check_vma=False)
```

```python
import math

import jax
import jax.numpy as jnp
import ml_dtypes
import numpy as np
from jax import lax
from jax.experimental import pallas as pl
from jax.experimental.pallas import tpu as pltpu
from jax.sharding import Mesh, PartitionSpec as P

BLOCK = 128
MODES = 16
SIDE = 4
OWNERS = SIDE * SIDE
f32 = jnp.float32
bf16 = jnp.bfloat16
SMALL = pltpu.CompilerParams(vmem_limit_bytes=16 << 20)


def split_pair(value):
    high = value.astype(bf16)
    return high, (value - high.astype(f32)).astype(bf16)


def transform_tables():
    steps = np.arange(BLOCK, dtype=np.float64)
    angles = 2.0 * math.pi / BLOCK * np.outer(steps, steps - 0.25)
    table = np.concatenate([np.cos(angles), -np.sin(angles)], axis=1)
    high = table.astype(np.float32).astype(ml_dtypes.bfloat16)
    low = (table - high.astype(np.float64)).astype(np.float32).astype(ml_dtypes.bfloat16)
    forward = np.concatenate([high.T, low.T], axis=1)
    backward = np.concatenate([high, low], axis=0)
    return jnp.asarray(forward), jnp.asarray(backward)


def mm(left, right):
    return lax.dot_general(left, right, (((1,), (0,)), ((), ())), preferred_element_type=f32)


def mm_nt(left, right, precision=None):
    return lax.dot_general(
        left, right, (((1,), (1,)), ((), ())), preferred_element_type=f32, precision=precision
    )


def full(shape):
    return pl.BlockSpec(shape, lambda *_: (0,) * len(shape))


def later(value, steps):
    moved = pltpu.roll(value, steps, 0)
    row = lax.broadcasted_iota(jnp.int32, (8, BLOCK), 0)
    return jnp.concatenate([jnp.where(row < steps, 0.0, moved[:8]), moved[8:]], axis=0)


def short_mix(block, rows, stream):
    return (
        rows[stream : stream + 1] * block
        + rows[3 + stream : 4 + stream] * later(block, 1)
        + rows[6 + stream : 7 + stream] * later(block, 2)
    )


def owner_rows(g):
    first = 512 * (g // SIDE) + 32 * (g % SIDE)
    return [slice(first + 128 * zl, first + 128 * zl + 32) for zl in range(SIDE)]


def owner_tile(x_ref, stream, g):
    return jnp.concatenate([x_ref[stream, span, :] for span in owner_rows(g)], axis=0)


def mix_kernel(
    mp_ref, x_hbm, taps_hbm, skip_hbm, residue_hbm, rate_hbm,
    product_hbm, head_ref, halo_ref, rows_ref, params_ref,
    x_ref, taps_ref, skip_ref, residue_ref, rate_ref, product_ref, small_sems, x_sems, out_sems,
):
    span = OWNERS * BLOCK
    at = pl.multiple_of(mp_ref[0] * span, span)
    small = [
        pltpu.make_async_copy(source, target, small_sems.at[i])
        for i, (source, target) in enumerate(
            (
                (taps_hbm.at[:, :, pl.ds(at, span)], taps_ref),
                (skip_hbm.at[:, pl.ds(at, span)], skip_ref),
                (residue_hbm, residue_ref),
                (rate_hbm, rate_ref),
            )
        )
    ]
    large = [
        [
            pltpu.make_async_copy(
                x_hbm.at[stream, pl.ds(512 * y, 512)],
                x_ref.at[stream, pl.ds(512 * y, 512)],
                x_sems.at[y, stream],
            )
            for stream in range(3)
        ]
        for y in range(SIDE)
    ]
    out = [
        pltpu.make_async_copy(
            product_ref.at[pl.ds(SIDE * y, SIDE)], product_hbm.at[pl.ds(SIDE * y, SIDE)], out_sems.at[y]
        )
        for y in range(SIDE)
    ]
    inner = [large[y][stream] for y in range(SIDE) for stream in (1, 2)]
    outer = [large[y][0] for y in range(SIDE)]
    for copy in small[:2] + inner + outer + small[2:]:
        copy.start()
    lane = lax.broadcasted_iota(jnp.int32, (16, BLOCK), 1) // 32
    small[0].wait()
    small[1].wait()
    for y in range(SIDE):
        table = jnp.concatenate(
            [taps_ref[lag, :, 512 * y : 512 * y + 512] for lag in range(3)]
            + [skip_ref[:, 512 * y : 512 * y + 512], jnp.zeros((6, 4 * BLOCK), f32)],
            axis=0,
        )
        for x in range(SIDE):
            rows = jnp.zeros((16, BLOCK), f32)
            for zl in range(SIDE):
                piece = table[:, zl * BLOCK : (zl + 1) * BLOCK]
                if zl != x:
                    piece = pltpu.roll(piece, (32 * (zl - x)) % BLOCK, 1)
                rows = jnp.where(lane == zl, piece, rows)
            rows_ref[SIDE * y + x] = rows
    for y in range(SIDE):
        large[y][1].wait()
        large[y][2].wait()
        for g in range(SIDE * y, SIDE * y + SIDE):
            rows = rows_ref[g]
            mixes = []
            for stream in (1, 2):
                block = owner_tile(x_ref, stream, g).T.astype(f32)
                halo_ref[g, 2 * stream : 2 * stream + 2, :] = block[BLOCK - 2 :].astype(bf16)
                mixes.append(short_mix(block, rows, stream))
                head_ref[stream - 1, g] = mixes[-1][:16]
            product_ref[g] = (mixes[0] * mixes[1]).astype(bf16)
        out[y].start()
    last = lax.broadcasted_iota(jnp.int32, (16, BLOCK), 0) + (BLOCK - 2)
    last = (last == lax.broadcasted_iota(jnp.int32, (16, BLOCK), 1)).astype(bf16)
    for y in range(SIDE):
        large[y][0].wait()
        for g in range(SIDE * y, SIDE * y + SIDE):
            halo_ref[g, 0:2, :] = mm_nt(last, owner_tile(x_ref, 0, g))[0:2].astype(bf16)
            halo_ref[g, 6:8, :] = jnp.zeros((2, BLOCK), bf16)
    small[2].wait()
    small[3].wait()
    rate = rate_ref[...]
    count = rate.shape[1]
    params_ref[...] = jnp.zeros((2 * MODES, BLOCK), f32)
    params_ref[:MODES, :count] = rate
    params_ref[MODES:, :count] = residue_ref[...] * jnp.sqrt(rate)
    for copy in out:
        copy.wait()


def in_hbm(value):
    return pltpu.with_memory_space_constraint(value, pltpu.HBM)


def mix_streams(projected, short_taps, skip_gain, residue, decay_rate, mp_index):
    span = OWNERS * BLOCK
    anywhere = pl.BlockSpec(memory_space=pl.ANY)
    whole = pl.BlockSpec(memory_space=pltpu.VMEM)
    mode_shape = residue.shape[::-1]
    return pl.pallas_call(
        mix_kernel,
        in_specs=[pl.BlockSpec(memory_space=pltpu.SMEM)] + [anywhere] * 5,
        out_specs=[anywhere] + [whole] * 4,
        out_shape=[
            jax.ShapeDtypeStruct((OWNERS, BLOCK, BLOCK), bf16),
            jax.ShapeDtypeStruct((2, OWNERS, 16, BLOCK), f32),
            jax.ShapeDtypeStruct((OWNERS, 8, BLOCK), bf16),
            jax.ShapeDtypeStruct((OWNERS, 16, BLOCK), f32),
            jax.ShapeDtypeStruct((2 * MODES, BLOCK), f32),
        ],
        scratch_shapes=[
            pltpu.VMEM(projected.shape, bf16),
            pltpu.VMEM((3, 3, span), f32),
            pltpu.VMEM((1, span), f32),
            pltpu.VMEM(mode_shape, f32),
            pltpu.VMEM(mode_shape, f32),
            pltpu.VMEM((OWNERS, BLOCK, BLOCK), bf16),
            pltpu.SemaphoreType.DMA((4,)),
            pltpu.SemaphoreType.DMA((SIDE, 3)),
            pltpu.SemaphoreType.DMA((SIDE,)),
        ],
        compiler_params=SMALL,
        name="mix",
    )(
        mp_index, in_hbm(projected), in_hbm(short_taps), in_hbm(skip_gain.reshape(1, -1)),
        in_hbm(residue.T), in_hbm(decay_rate.T),
    )


def halo_term(halo, rows, stream):
    at = lax.broadcasted_iota(jnp.int32, (16, BLOCK), 0)
    older = halo[2 * stream : 2 * stream + 1]
    newer = halo[2 * stream + 1 : 2 * stream + 2]
    one = rows[3 + stream : 4 + stream]
    two = rows[6 + stream : 7 + stream]
    return jnp.where(at == 0, one * newer + two * older, jnp.where(at == 1, two * newer, 0.0))


def head_kernel(product_ref, head_ref, halo_ref, rows_ref, out_ref):
    del product_ref
    for g in range(OWNERS):
        halo = halo_ref[g].astype(f32)
        rows = rows_ref[g]
        k_mix = head_ref[0, g] + halo_term(halo, rows, 1)
        v_mix = head_ref[1, g] + halo_term(halo, rows, 2)
        out_ref[g] = (k_mix * v_mix).astype(bf16)


def finish_product(product, head, halo, rows):
    return pl.pallas_call(
        head_kernel,
        grid=(1,),
        in_specs=[
            pl.BlockSpec(memory_space=pl.ANY), full(head.shape), full(halo.shape), full(rows.shape)
        ],
        out_specs=pl.BlockSpec((OWNERS, 16, BLOCK), lambda i: (0, 0, 0)),
        out_shape=jax.ShapeDtypeStruct(product.shape, bf16),
        input_output_aliases={0: 0},
        compiler_params=SMALL,
        name="head",
    )(product, head, halo, rows)


def prepare_kernel(q_ref, product_ref, halo_ref, rows_ref, mix_ref, direct_ref):
    for x in range(SIDE):
        rows = rows_ref[x]
        mix = short_mix(owner_tile(q_ref, 0, x).T.astype(f32), rows, 0)
        mix_ref[x, :16, :] = mix[:16] + halo_term(halo_ref[x].astype(f32), rows, 0)
        mix_ref[x, 16:, :] = mix[16:]
        direct_ref[x] = rows[9:10] * product_ref[x].astype(f32)


def prepare_gate(projected, product, halo, rows):
    tile = lambda n: pl.BlockSpec((4, n, BLOCK), lambda i: (i, 0, 0))
    return pl.pallas_call(
        prepare_kernel,
        grid=(4,),
        in_specs=[
            pl.BlockSpec((1, 512, BLOCK), lambda i: (0, i, 0)), tile(BLOCK), tile(8), tile(16)
        ],
        out_specs=[tile(BLOCK), tile(BLOCK)],
        out_shape=[jax.ShapeDtypeStruct(product.shape, f32)] * 2,
        compiler_params=SMALL,
        name="prepare",
    )(in_hbm(projected), product, halo, rows)


def gate_kernel(mix_ref, direct_ref, long_ref, out_hbm, out_ref, sems):
    copies = [
        pltpu.make_async_copy(
            out_ref.at[pl.ds(512 * y, 512)], out_hbm.at[pl.ds(512 * y, 512)], sems.at[y]
        )
        for y in range(SIDE)
    ]
    for g in range(OWNERS):
        gated = (mix_ref[g] * (long_ref[g].astype(f32) + direct_ref[g])).astype(bf16).T
        for zl, span in enumerate(owner_rows(g)):
            out_ref[span, :] = gated[32 * zl : 32 * zl + 32]
        if g % SIDE == SIDE - 1:
            copies[g // SIDE].start()
    for copy in copies:
        copy.wait()


def apply_gate(mix, direct, long_part):
    shape = (OWNERS * BLOCK, BLOCK)
    return pl.pallas_call(
        gate_kernel,
        in_specs=[pl.BlockSpec(memory_space=pltpu.VMEM)] * 3,
        out_specs=pl.BlockSpec(memory_space=pl.ANY),
        out_shape=jax.ShapeDtypeStruct(shape, bf16),
        scratch_shapes=[pltpu.VMEM(shape, bf16), pltpu.SemaphoreType.DMA((SIDE,))],
        compiler_params=SMALL,
        name="gate",
    )(mix, direct, long_part)


def table_kernel(
    zl_ref, p0_ref, p1_ref, p2_ref, p3_ref, forward_ref,
    spec_ref, step_ref, tail_ref, start_ref, decay_ref,
):
    params = (
        p0_ref[...]
        + pltpu.roll(p1_ref[...], 32, 1)
        + pltpu.roll(p2_ref[...], 64, 1)
        + pltpu.roll(p3_ref[...], 96, 1)
    )
    params = pltpu.roll(params, zl_ref[0] * 32, 1)
    rate = params[:MODES]
    weight = params[MODES:]
    decay_ref[...] = jnp.exp(-float(BLOCK) * rate)
    place = lax.broadcasted_iota(jnp.int32, (BLOCK, BLOCK), 0).astype(f32)
    row = lax.broadcasted_iota(jnp.int32, (8, BLOCK), 0).astype(f32)
    kernel = jnp.zeros((BLOCK, BLOCK), f32)
    for n in range(MODES):
        own = rate[n : n + 1]
        gain = weight[n : n + 1]
        kernel = kernel + gain * jnp.exp(-own * place)
        step_ref[n] = jnp.broadcast_to(jnp.exp(-8.0 * own), (8, BLOCK))
        tail_ref[n] = jnp.exp(-own * (7.0 - row))
        start_ref[n] = gain * jnp.exp(-own * (row + 1.0))
    high, low = split_pair(kernel)
    table = forward_ref[...]
    spec = mm(table, jnp.concatenate([high, high], axis=0)) + mm(table[:, :BLOCK], low)
    spec = spec * (1.0 / BLOCK)
    spec_ref[...] = jnp.concatenate([spec, spec], axis=1)


def make_tables(pieces, forward, zl_index):
    part = jax.ShapeDtypeStruct((MODES, 8, BLOCK), f32)
    return pl.pallas_call(
        table_kernel,
        grid_spec=pltpu.PrefetchScalarGridSpec(
            num_scalar_prefetch=1,
            grid=(1,),
            in_specs=[full((2 * MODES, BLOCK))] * 4 + [full(forward.shape)],
            out_specs=[full((2 * BLOCK, 2 * BLOCK))] + [full(part.shape)] * 3 + [full((MODES, BLOCK))],
        ),
        out_shape=[
            jax.ShapeDtypeStruct((2 * BLOCK, 2 * BLOCK), f32), part, part, part,
            jax.ShapeDtypeStruct((MODES, BLOCK), f32),
        ],
        compiler_params=SMALL,
        name="tables",
    )(zl_index, *pieces, forward)


def state_kernel(x_ref, step_ref, tail_ref, decay_ref, state_ref, run_ref):
    step = step_ref[...]
    tail = tail_ref[...]

    def one_block(b, carry):
        x = x_ref[b].astype(f32)
        state = jnp.zeros((MODES, 8, BLOCK), f32)
        for i in range(BLOCK // 8):
            state = state * step + x[8 * i : 8 * i + 8][None]
        state_ref[b] = jnp.sum(state * tail, axis=1)
        return carry

    lax.fori_loop(0, OWNERS, one_block, 0)
    decay = decay_ref[...]
    for y in range(SIDE):
        run = state_ref[SIDE * y]
        for x in range(1, SIDE):
            run = run * decay + state_ref[SIDE * y + x]
        run_ref[y] = run


def block_states(blocks, step, tail, decay):
    return pl.pallas_call(
        state_kernel,
        out_shape=[
            jax.ShapeDtypeStruct((OWNERS, MODES, BLOCK), f32),
            jax.ShapeDtypeStruct((SIDE, MODES, BLOCK), f32),
        ],
        compiler_params=SMALL,
        name="states",
    )(blocks, step, tail, decay)


def conv_kernel(x_ref, spec_ref, forward_ref, backward_ref, out_ref):
    for pair in range(OWNERS // 2):
        x = jnp.concatenate([x_ref[2 * pair], x_ref[2 * pair + 1]], axis=1)
        turned = mm(forward_ref[...], jnp.concatenate([x, x], axis=0))
        x_re, x_im = turned[:BLOCK], turned[BLOCK:]
        k_re, k_im = spec_ref[:BLOCK, :], spec_ref[BLOCK:, :]
        mixed = jnp.concatenate([x_re * k_re - x_im * k_im, x_re * k_im + x_im * k_re], axis=0)
        high, low = split_pair(mixed)
        both = mm(backward_ref[...], high)
        result = both[:BLOCK] + both[BLOCK:] + mm(backward_ref[:BLOCK, :], low)
        out_ref[2 * pair] = result[:, :BLOCK]
        out_ref[2 * pair + 1] = result[:, BLOCK:]


def convolve_blocks(blocks, spec, forward, backward):
    return pl.pallas_call(
        conv_kernel,
        out_shape=jax.ShapeDtypeStruct(blocks.shape, f32),
        compiler_params=SMALL,
        name="conv",
    )(blocks, spec, forward, backward)


def readout_kernel(
    zl_ref, inner_ref, state_ref, r0_ref, r1_ref, r2_ref, r3_ref, step_ref, start_ref, decay_ref,
    out_ref, runs_ref, enter_ref,
):
    own = zl_ref[0]
    for k, ref in enumerate((r0_ref, r1_ref, r2_ref, r3_ref)):
        runs_ref[(own + k) % SIDE] = ref[...]
    decay = decay_ref[...]
    squared = decay * decay
    run_decay = squared * squared
    state = jnp.zeros((MODES, BLOCK), f32)
    for y in range(SIDE):
        for zl in range(SIDE):

            @pl.when(own == zl)
            def _(state=state, y=y):
                enter_ref[SIDE * y] = state

            state = state * run_decay + runs_ref[zl, y]
        inside = enter_ref[SIDE * y]
        for x in range(1, SIDE):
            inside = inside * decay + state_ref[SIDE * y + x - 1]
            enter_ref[SIDE * y + x] = inside
    step = step_ref[...]

    def one_block(b, carry):
        share = start_ref[...] * enter_ref[b][:, None, :]
        for i in range(BLOCK // 16):
            parts = []
            for half in range(2):
                at = 16 * i + 8 * half
                parts.append(inner_ref[b, at : at + 8, :] + jnp.sum(share, axis=0))
                share = share * step
            out_ref[b, 16 * i : 16 * i + 16, :] = jnp.concatenate(parts, axis=0).astype(bf16)
        return carry

    lax.fori_loop(0, OWNERS, one_block, 0)


def add_states(inner, states, runs, step, start, decay, zl_index):
    return pl.pallas_call(
        readout_kernel,
        grid_spec=pltpu.PrefetchScalarGridSpec(
            num_scalar_prefetch=1,
            grid=(1,),
            in_specs=[full(inner.shape), full(states.shape)]
            + [full((SIDE, MODES, BLOCK))] * 4
            + [full(step.shape)] * 2
            + [full(decay.shape)],
            out_specs=full(inner.shape),
            scratch_shapes=[
                pltpu.VMEM((SIDE, SIDE, MODES, BLOCK), f32),
                pltpu.VMEM((OWNERS, MODES, BLOCK), f32),
            ],
        ),
        out_shape=jax.ShapeDtypeStruct(inner.shape, bf16),
        compiler_params=SMALL,
        name="readout",
    )(zl_index, inner, states, *runs, step, start, decay)


def body(projected, short_taps, skip_gain, residue, decay_rate):
    mp_index = lax.axis_index("mp").astype(jnp.int32).reshape(1)
    zl_index = lax.axis_index("zl").astype(jnp.int32).reshape(1)
    count = SIDE ** 3

    def from_zl(value, k):
        return lax.ppermute(value, "zl", [(zl, (zl - k) % SIDE) for zl in range(SIDE)])

    product, head, halo, rows, params = mix_streams(
        projected, short_taps, skip_gain, residue, decay_rate, mp_index
    )
    halo = lax.ppermute(halo, ("y", "zl", "x"), [(i, i + 1) for i in range(count - 1)])
    pieces = [params] + [from_zl(params, k) for k in range(1, SIDE)]
    product = finish_product(product, head, halo, rows)
    product, pieces[3] = lax.optimization_barrier((product, pieces[3]))
    blocks = lax.all_to_all(product, ("y", "x"), split_axis=0, concat_axis=0, tiled=True)
    gate_mix, direct = prepare_gate(projected, product, halo, rows)
    blocks, gate_mix, direct = lax.optimization_barrier((blocks, gate_mix, direct))
    forward, backward = transform_tables()
    spec, step, tail, start, decay = make_tables(pieces, forward, zl_index)
    states, run = block_states(blocks, step, tail, decay)
    arriving = {k: from_zl(run, k) for k in range(SIDE - 1, 0, -1)}
    runs = [run] + [arriving[k] for k in range(1, SIDE)]
    inner = convolve_blocks(blocks, spec, forward, backward)
    result = add_states(inner, states, runs, step, start, decay, zl_index)
    long_part = lax.all_to_all(result, ("y", "x"), split_axis=0, concat_axis=0, tiled=True)
    return apply_gate(gate_mix, direct, long_part)


def solution(mesh):
    split = Mesh(mesh.devices.reshape(SIDE, SIDE, SIDE, -1), ("y", "zl", "x", "mp"))
    seq = ("y", "zl", "x")
    in_specs = (P(None, "mp", seq), P(), P(), P(seq, None), P(seq, None))
    out_specs = P("mp", seq)
    return jax.shard_map(body, mesh=split, in_specs=in_specs, out_specs=out_specs, check_vma=False)
```
